256 devices in a mesh: dp: 32 (over x, z_lo, y), tensor: 8 (over z_hi, core).
Axes of the slice: x: 4, y: 4, z: 8 (z_hi: 4, z_lo: 2; z = z_hi * 2 + z_lo), core: 2. Of those that a mesh axis runs over, the one named last changes fastest.
Arguments:
- gradient: bfloat16 [2, 2048, 16384], P(None, 'dp', 'tensor'), may hold values from -1000 to 1000
- master: float32 [2, 2048, 16384], P(None, 'dp', 'tensor'), may hold values from -0.046875 to 0.046875
- first_moment: float32 [2, 2048, 16384], P(None, 'dp', 'tensor'), may hold values from -3 to 3
- second_moment: float32 [2, 2048, 16384], P(None, 'dp', 'tensor'), may hold values from 0.05 to 1
- residual: bfloat16 [8192, 16384], P('dp', 'tensor'), may hold values from -1500 to 1500
- norm_gain: float32 [16384], replicated, may hold values from 0.5 to 2
- queries: bfloat16 [8192, 128, 128], P('dp', 'tensor'), may hold values from -170 to 170
- layer_cache: bfloat16 [8192, 2, 8, 32, 128], P('dp', None, 'tensor'), may hold values from -4.5 to 4.5
- fresh_entries: bfloat16 [8192, 2, 8, 128], P('dp', None, 'tensor'), may hold values from -6 to 6
- lengths: int32 [8192], P('dp'), may hold values from 2 to 32, as said below
- shard_table: int32 [32], replicated, may hold values from 0 to 31, each once
Outputs:
- new_first: float32 [2, 2048, 16384], P(None, 'dp', 'tensor')
- new_second: float32 [2, 2048, 16384], P(None, 'dp', 'tensor')
- attended: bfloat16 [8192, 128, 128], P('dp', 'tensor')
- activated: bfloat16 [8192, 2048], P('dp', 'tensor')
The draws below stay inside these ranges and needn't reach their ends.
Inputs may be any that keep to these rules, and one draw needn't show every extreme that they name: `lengths`: every row has 2 or more valid positions, and in each rollout group's rows one row has all 32. `shard_table`: A permutation of the learner shards.
All inputs are finite; a program needn't handle non-finite values.
Results may differ from the reference program's by a relative error of at most 0.0072.
Values may be sent and summed in bfloat16 or wider, within the bound.
A program may use at most 128 MiB of HBM per device.

```python
import math
import jax
import jax.numpy as jnp
from jax import lax

D = 16384
HQ = 128
KVH = 8
HD = 128
UNITS_DEV = 8
ROWS_DEV = 256
CACHE = 32
ROWS = 8192
SLAB = 2048
N_DP = 32
N_TENSOR = 8


def spread_scales(key, count):
    return 10.0 ** jax.random.uniform(key, (count,), jnp.float32)


def draw_gradient(key, part):
    base_key, column_key = jax.random.split(jax.random.fold_in(key, 1), 2)
    loud_key = jax.random.fold_in(key, 21)
    rising = 10.0 ** (jnp.arange(SLAB, dtype=jnp.float32) / SLAB)
    columns = spread_scales(column_key, D)
    loudness = 10.0 ** jax.random.uniform(loud_key, (N_DP, N_TENSOR), jnp.float32, -1.0, 0.0)
    entries = jnp.clip(jax.random.normal(base_key, (2, SLAB, D), jnp.float32), -6.0, 6.0)
    entries = entries * rising[None, :, None] * columns[None, None, :]
    blocked = entries.reshape(2, N_DP, SLAB // N_DP, N_TENSOR, D // N_TENSOR)
    blocked = blocked * loudness[None, :, None, :, None]
    return blocked.reshape(2, SLAB, D).astype(jnp.bfloat16)


def draw_residual(key, part):
    base_key, row_key, column_key = jax.random.split(jax.random.fold_in(key, 2), 3)
    row_scales = spread_scales(row_key, ROWS)
    columns = spread_scales(column_key, D)
    entries = jnp.clip(jax.random.normal(base_key, (ROWS, D), jnp.float32), -6.0, 6.0)
    return (entries * row_scales[:, None] * columns[None, :]).astype(jnp.bfloat16)


def draw_layer_cache(key, part):
    entries = jnp.clip(jax.random.normal(jax.random.fold_in(key, 3), (ROWS, 2, KVH, CACHE, HD), jnp.float32), -4.5, 4.5)
    return entries.astype(jnp.bfloat16)


def draw_queries(key, part):
    entries = jnp.clip(jax.random.normal(jax.random.fold_in(key, 5), (ROWS, HQ, HD), jnp.float32), -4.5, 4.5)
    return entries.astype(jnp.bfloat16)


def draw_lengths(key, part):
    drawn_lengths = jax.random.randint(jax.random.fold_in(key, 4), (ROWS,), 2, CACHE + 1)
    full_rows = jnp.arange(ROWS) % ROWS_DEV == 0
    return jnp.where(full_rows, CACHE, drawn_lengths).astype(jnp.int32)


def block_levels(key, shape, shards, smallest, largest):
    factor_of, own = 1.0, jax.random.fold_in(key, 6)
    for position, shards_of in shards:
        heights = jnp.exp(jax.random.uniform(jax.random.fold_in(own, position), (shards_of,), jnp.float32, smallest / len(shards), largest / len(shards)))
        factor_of = factor_of * jnp.repeat(heights, shape[position] // shards_of).reshape([-1 if axis == position else 1 for axis in range(len(shape))])
    return factor_of


def scatter_about(key, dims, scale, most, pieces=(), kind=jnp.bfloat16):
    values = jax.random.normal(key, dims, jnp.float32) * scale
    if len(pieces) > 0:
        values = block_levels(key, dims, pieces, -0.22, 0.18) * values
    return jnp.clip(values, min=-most, max=most).astype(kind)


def setup_inputs(seed: int = 0) -> dict:
    streams_of = jax.random.split(jax.random.key(seed), 12)
    gradient = draw_gradient(jax.random.fold_in(streams_of[11], 71), 0)
    master = scatter_about(streams_of[1], (2, SLAB, D), D ** -0.5, 0.046875, ((1, 32), (2, 8)), jnp.float32)
    first_moment = scatter_about(streams_of[2], (2, SLAB, D), 0.5, 3.0, ((1, 32), (2, 8)), jnp.float32)
    second_moment = jnp.clip(jnp.exp(math.log(1.0) - 2.9957323 * jax.random.uniform(streams_of[3], (2, SLAB, D), jnp.float32) ** block_levels(streams_of[3], (2, SLAB, D), ((1, 32), (2, 8)), -0.2, 0.2)), 0.05, 1.0)
    residual = draw_residual(jax.random.fold_in(streams_of[11], 71), 0)
    norm_gain = jnp.clip(jnp.exp(jax.random.uniform(streams_of[5], (D,), jnp.float32, math.log(0.5), math.log(2.0))), 0.5, 2.0)
    queries = draw_queries(jax.random.fold_in(streams_of[11], 71), 0)
    layer_cache = draw_layer_cache(jax.random.fold_in(streams_of[11], 71), 0)
    fresh_entries = scatter_about(streams_of[8], (ROWS, 2, KVH, HD), 1.0, 6.0, ((0, 32), (2, 8)))
    lengths = draw_lengths(jax.random.fold_in(streams_of[11], 71), 0)
    shard_table = jax.random.permutation(streams_of[10], N_DP).astype(jnp.int32)
    return dict(gradient=gradient, master=master, first_moment=first_moment, second_moment=second_moment, residual=residual, norm_gain=norm_gain, queries=queries, layer_cache=layer_cache, fresh_entries=fresh_entries, lengths=lengths, shard_table=shard_table)


LEARN_RATE = 0.001
CLIP_LEVEL = 0.5
CLIP_EPSILON = 1e-06
FIRST_DECAY = 0.9
SECOND_DECAY = 0.95
FIRST_CORRECTION = 1.0 - 0.9 ** 10
SECOND_CORRECTION = 1.0 - 0.95 ** 10
ADAM_EPSILON = 1e-08
NORM_EPSILON = 1e-05

def attend(queries, layer_cache, fresh_entries, lengths):
    row_count, head_count, head_width = queries.shape
    group_count = layer_cache.shape[2]
    per_group = head_count // group_count
    score_scale = 1.0 / math.sqrt(head_width)
    grouped = queries.reshape(row_count, group_count, per_group, head_width).astype(jnp.float32)
    cached_keys = layer_cache[:, 0].astype(jnp.float32)
    cached_values = layer_cache[:, 1].astype(jnp.float32)
    scores = jnp.einsum('rghd,rgpd->rghp', grouped, cached_keys) * score_scale
    own_score = jnp.einsum('rghd,rgd->rgh', grouped, fresh_entries[:, 0].astype(jnp.float32)) * score_scale
    positions = lax.broadcasted_iota(jnp.int32, (row_count, 1, 1, cached_keys.shape[2]), 3)
    in_range = positions < lengths.astype(jnp.int32)[:, None, None, None]
    scores = jnp.where(in_range, scores, -jnp.inf)
    row_peak = jnp.maximum(lax.optimization_barrier(jnp.max(scores, axis=3)), own_score)
    cached_exp = jnp.exp(scores - row_peak[..., None])
    own_exp = jnp.exp(own_score - row_peak)
    denominator = lax.optimization_barrier(jnp.sum(cached_exp, axis=3)) + own_exp
    cached_prob = (cached_exp / denominator[..., None]).astype(jnp.bfloat16).astype(jnp.float32)
    own_prob = (own_exp / denominator).astype(jnp.bfloat16).astype(jnp.float32)
    combined = jnp.einsum('rghp,rgpd->rghd', cached_prob, cached_values)
    combined = combined + own_prob[..., None] * fresh_entries[:, 1].astype(jnp.float32)[:, :, None, :]
    return combined.reshape(row_count, head_count, head_width).astype(jnp.bfloat16)

def reference(gradient, master, first_moment, second_moment, residual, norm_gain, queries, layer_cache, fresh_entries, lengths, shard_table):
    gradient_wide = gradient.astype(jnp.float32)
    total_sum = jnp.sum(gradient_wide * gradient_wide)
    clip_limit = CLIP_LEVEL * math.sqrt(gradient.size)
    clip_factor = jnp.minimum(1.0, clip_limit / (jnp.sqrt(total_sum) + CLIP_EPSILON))
    clipped = gradient_wide * clip_factor
    new_first = FIRST_DECAY * first_moment + (1.0 - FIRST_DECAY) * clipped
    new_second = SECOND_DECAY * second_moment + (1.0 - SECOND_DECAY) * clipped * clipped
    adam_step = new_first / FIRST_CORRECTION / (jnp.sqrt(new_second / SECOND_CORRECTION) + ADAM_EPSILON)
    fresh_weight = (master - LEARN_RATE * adam_step).astype(jnp.bfloat16)
    residual_wide = residual.astype(jnp.float32)
    mean_square = lax.optimization_barrier(jnp.mean(residual_wide * residual_wide, axis=1, keepdims=True))
    normed = (residual_wide * lax.rsqrt(mean_square + NORM_EPSILON) * norm_gain).astype(jnp.bfloat16)
    normed_wide = normed.astype(jnp.float32)
    gate_sum = jnp.dot(normed_wide, fresh_weight[0].astype(jnp.float32).T, precision=lax.Precision.HIGHEST)
    up_sum = jnp.dot(normed_wide, fresh_weight[1].astype(jnp.float32).T, precision=lax.Precision.HIGHEST)
    hidden = jax.nn.silu(gate_sum) * up_sum
    blocks = hidden.reshape(ROWS, N_DP, N_TENSOR, UNITS_DEV)
    ordered = jnp.take(blocks, shard_table.astype(jnp.int32), axis=1)
    activated = jnp.transpose(ordered, (0, 2, 1, 3)).reshape(ROWS, SLAB).astype(jnp.bfloat16)

    def attend_block(block):
        return attend(block[0], block[1], block[2], block[3])
    attended = lax.map(attend_block, (queries.reshape(N_DP, ROWS_DEV, HQ, HD), layer_cache.reshape(N_DP, ROWS_DEV, 2, KVH, CACHE, HD), fresh_entries.reshape(N_DP, ROWS_DEV, 2, KVH, HD), lengths.reshape(N_DP, ROWS_DEV)))
    attended = attended.reshape(ROWS, HQ, HD)
    return (new_first, new_second, attended, activated)
```

```python
import math

import jax
import jax.numpy as jnp
from jax import lax
from jax.experimental import pallas as pl
from jax.experimental.pallas import tpu as pltpu
from jax.sharding import PartitionSpec as P

LEARN_RATE = 0.001
CLIP_LEVEL = 0.5
CLIP_EPSILON = 1e-06
FIRST_DECAY = 0.9
SECOND_DECAY = 0.95
FIRST_CORRECTION = 1.0 - 0.9**10
SECOND_CORRECTION = 1.0 - 0.95**10
ADAM_EPSILON = 1e-08
NORM_EPSILON = 1e-05

MESH = pl.DeviceIdType.MESH
F32 = jnp.float32
BF16 = jnp.bfloat16

K_DEV = 2048
ROWS = 256
UNITS = 64
WIDTH = 16384


class Remote:
    def __init__(self, src, dst, sends, recvs, slot, device, arrives=None):
        self.copy = pltpu.make_async_remote_copy(
            src_ref=src, dst_ref=dst, send_sem=sends.at[slot], recv_sem=recvs.at[slot],
            device_id=device, device_id_type=MESH)
        arrives = dst if arrives is None else arrives
        self.inbound = pltpu.make_async_remote_copy(
            src_ref=arrives, dst_ref=arrives, send_sem=sends.at[slot], recv_sem=recvs.at[slot],
            device_id=device, device_id_type=MESH)
        self.copy.start()

    def sent(self):
        self.copy.wait_send()

    def came(self):
        self.inbound.wait_recv()


N_COPIES = 56


def step_kernel(
    clip_limit,
    grad_h, master_h, first_h, second_h, resid_h, gain_h, table_ref,
    act_ref, clip_ref,
    g_v, ma_v, m_v, v_v, gf, gain_v, a_v, b_v, b_swap, c_s, c_r, h_s, h_r,
    p_s, p_r, t_s, t_r, s_g, load_sem, sends, recvs, many,
):
    d = lax.axis_index("dp")
    t = lax.axis_index("tensor")
    x, zl, y = d // 8, (d // 4) % 2, d % 4
    zh, c = t // 2, t % 2
    oc = 1 - c
    xp, xq = x + 1 - 2 * (x % 2), (x + 3 + 2 * (x % 2)) % 4
    yp, yq = y + 1 - 2 * (y % 2), (y + 3 + 2 * (y % 2)) % 4

    def at(x_, zl_, y_, zh_=None, c_=None):
        zh_ = zh if zh_ is None else zh_
        c_ = c if c_ is None else c_
        return {"dp": x_ * 8 + zl_ * 4 + y_, "tensor": zh_ * 2 + c_}

    to_xp, to_yp, to_diag = at(xp, zl, y), at(x, zl, yp), at(xp, zl, yp)
    to_xq, to_yq, to_zl = at(xq, zl, y), at(x, zl, yq), at(x, 1 - zl, y)
    to_core = at(x, zl, y, zh, oc)

    barrier = pltpu.get_barrier_semaphore()
    for k in range(1, 8):
        pl.semaphore_signal(barrier, inc=1, device_id={"dp": d, "tensor": (t + k) % 8}, device_id_type=MESH)
    for k in range(1, 32):
        pl.semaphore_signal(barrier, inc=1, device_id={"dp": (d + k) % 32, "tensor": t}, device_id_type=MESH)

    loads = [
        pltpu.make_async_copy(grad_h, g_v, load_sem.at[0]),
        pltpu.make_async_copy(resid_h, a_v.at[0, c], load_sem.at[1]),
        pltpu.make_async_copy(gain_h.at[pl.ds(pl.multiple_of(t * 16, 16), 16)], gain_v, load_sem.at[2]),
        pltpu.make_async_copy(master_h, ma_v, load_sem.at[3]),
        pltpu.make_async_copy(first_h, m_v, load_sem.at[4]),
        pltpu.make_async_copy(second_h, v_v, load_sem.at[5]),
    ]
    for load in loads:
        load.start()

    used = []

    def remote(src, dst, device, arrives=None):
        r = Remote(src, dst, sends, recvs, len(used), device, arrives)
        used.append(r)
        return r

    loads[0].wait()

    def square(i, acc):
        g = g_v[i // 4, pl.ds(pl.multiple_of((i % 4) * 16, 16), 16), :].astype(F32)
        gf[i // 4, pl.ds(pl.multiple_of((i % 4) * 16, 16), 16), :] = g
        sq = g * g
        return acc + (sq[:8] + sq[8:])

    acc = lax.fori_loop(0, 8, square, jnp.zeros((8, K_DEV), F32))
    local = jnp.sum(jnp.sum(acc, axis=0, keepdims=True), axis=1, keepdims=True)
    p_s[...] = jnp.broadcast_to(local, (8, 128))

    pl.semaphore_wait(barrier, 38)

    for k in range(1, 32):
        pltpu.make_async_remote_copy(
            src_ref=p_s, dst_ref=p_r.at[k - 1], send_sem=many.at[0], recv_sem=many.at[1],
            device_id={"dp": (d + k) % 32, "tensor": t}, device_id_type=MESH).start()

    loads[1].wait()
    ones = jnp.ones((8, 512), BF16)
    row_squares = jnp.zeros((8, ROWS), F32)
    for k in range(4):
        r = a_v[0, c, :, k * 512:(k + 1) * 512].astype(F32)
        sq = r * r
        high = sq.astype(BF16)
        low = (sq - high.astype(F32)).astype(BF16)
        for part in (high, low):
            row_squares += lax.dot_general(ones, part, (((1,), (1,)), ((), ())), preferred_element_type=F32)

    everyone = pltpu.make_async_remote_copy(
        src_ref=p_r, dst_ref=p_r, send_sem=many.at[0], recv_sem=many.at[1],
        device_id=to_core, device_id_type=MESH)
    everyone.wait_send()
    everyone.wait_recv()
    total = p_s[...]
    for k in range(31):
        total += p_r[k]
    t_s[:, :128] = total
    t_s[:, 128:] = row_squares

    for k in range(1, 8):
        pltpu.make_async_remote_copy(
            src_ref=t_s, dst_ref=t_r.at[k - 1], send_sem=many.at[2], recv_sem=many.at[3],
            device_id={"dp": d, "tensor": (t + k) % 8}, device_id_type=MESH).start()

    def rows_of(slot, half, r):
        return a_v.at[slot, half, pl.ds(r * 128, 128)]

    def to_other_core(slot, r):
        return remote(rows_of(slot, c, r), rows_of(slot, c, r), to_core, rows_of(slot, oc, r))

    rows_x = [remote(rows_of(0, c, r), rows_of(1, c, r), to_xp) for r in range(2)]
    rows_y = [remote(rows_of(0, c, r), rows_of(2, c, r), to_yp) for r in range(2)]
    core_rows = [to_other_core(0, 0), to_other_core(0, 1)]

    team = pltpu.make_async_remote_copy(
        src_ref=t_r, dst_ref=t_r, send_sem=many.at[2], recv_sem=many.at[3],
        device_id=to_core, device_id_type=MESH)
    team.wait_send()
    team.wait_recv()
    both = t_s[...]
    for k in range(7):
        both += t_r[k]
    clip = jnp.minimum(1.0, clip_limit / (jnp.sqrt(both[:, :128]) + CLIP_EPSILON))
    clip_ref[...] = clip
    s_g[0] = both[:, 128:]
    square_copies = [remote(s_g.at[0], s_g.at[slot], device) for slot, device in ((1, to_xp), (2, to_yp), (3, to_diag))]

    for load in loads[2:]:
        load.wait()
    clip_one = clip[0:1, 0:1]
    gain = jnp.concatenate([gain_v[i:i + 1, :] for i in range(16)], axis=1)

    def fresh(parity, zone):
        row = pl.multiple_of((2 * zone + parity) * 8, 8)
        parts = []
        for i in range(2):
            clipped = gf[i, pl.ds(row, 8), :] * clip_one
            new_first = FIRST_DECAY * m_v[i, pl.ds(row, 8), :] + (1.0 - FIRST_DECAY) * clipped
            new_second = SECOND_DECAY * v_v[i, pl.ds(row, 8), :] + (1.0 - SECOND_DECAY) * clipped * clipped
            step = (new_first * (LEARN_RATE / FIRST_CORRECTION)) / (
                jnp.sqrt(new_second * (1.0 / SECOND_CORRECTION)) + ADAM_EPSILON)
            parts.append((ma_v[i, pl.ds(row, 8), :] - step) * gain)
        return jnp.concatenate(parts, axis=0).astype(BF16)

    @pl.loop(0, 4)
    def _(zone):
        b_swap[pl.ds(pl.multiple_of(zone * 16, 16), 16), :] = fresh(oc, zone)

    swap = remote(b_swap, b_v.at[0, c], to_core, b_v.at[0, oc])

    @pl.loop(0, 4)
    def _(zone):
        b_v[0, c, pl.ds(pl.multiple_of(zone * 16, 16), 16), :] = fresh(c, zone)

    def piece(slot, k):
        return b_v.at[slot, c if k == 0 else oc]

    def units(src, dst, k, device):
        return remote(piece(src, k), piece(dst, k), device)

    unit = {}
    for k in range(2):
        if k == 1:
            swap.came()
        unit[1, k] = units(0, 1, k, to_zl)
        unit[2, k] = units(0, 2, k, to_xq)
        unit[4, k] = units(0, 4, k, to_yq)

    core_got = []
    diag = []

    def pass_rows(r):
        rows_x[r].came()
        core_got.append(to_other_core(1, r))
        if r == 0:
            diag.append(remote(rows_of(1, c, 0), rows_of(3, c, 0), to_yp))
        rows_y[r].came()
        core_got.append(to_other_core(2, r))
        if r == 1:
            diag.append(remote(rows_of(2, c, 1), rows_of(3, c, 1), to_xp))

    pass_rows(0)
    for k in range(2):
        unit[1, k].came()
        unit[3, k] = units(1, 3, k, to_xq)
        unit[5, k] = units(1, 5, k, to_yq)
    unit[2, 0].came()
    unit[6, 0] = units(2, 6, 0, to_yq)
    unit[4, 0].came()
    unit[4, 1].came()
    unit[6, 1] = units(4, 6, 1, to_xq)
    unit[2, 1].came()
    pass_rows(1)
    for r in core_rows + core_got:
        r.came()

    def product(slot, count, a):
        out = jnp.zeros((count * UNITS, ROWS), F32)
        for h in range(2):
            lhs = b_v[slot:slot + count, h].reshape(count * UNITS, K_DEV)
            out += lax.dot_general(lhs, a_v[a, h], (((1,), (1,)), ((), ())), preferred_element_type=F32)
        return out.reshape(count, 4, 16, ROWS).astype(BF16)

    def pair_tile(p, a):
        out = product(2 * p, 2, a)
        for z in range(4):
            c_s[p, z, a] = out[:, z]

    sums = []

    def send_sums(view_s, view_r):
        for k in range(1, 4):
            z = (zh + k) % 4
            sums.append(remote(view_s(z), view_r(k - 1), at(x, zl, y, z, c)))

    def pair_three(p):
        @pl.loop(0, 3)
        def _(a):
            pair_tile(p, a)

        send_sums(lambda z: c_s.at[p, z, pl.ds(0, 3)], lambda k: c_r.at[k, p, pl.ds(0, 3)])

    pair_three(0)
    unit[3, 0].came()
    unit[7, 0] = units(3, 7, 0, to_yq)
    unit[5, 0].came()
    unit[5, 1].came()
    unit[7, 1] = units(5, 7, 1, to_xq)
    unit[3, 1].came()
    pair_three(1)
    pair_three(2)
    last_rows = []
    for r in range(2):
        diag[r].came()
        last_rows.append(to_other_core(3, r))
    for r in last_rows:
        r.came()
    for p in range(3):
        pair_tile(p, 3)
    send_sums(lambda z: c_s.at[pl.ds(0, 3), z, 3], lambda k: c_r.at[k, pl.ds(0, 3), 3])

    for q in range(2):
        for k in range(2):
            unit[6 + q, k].came()

        @pl.loop(0, 4)
        def _(a):
            out = product(6 + q, 1, a)
            for z in range(4):
                c_s[3, z, a, q] = out[0, z]

        send_sums(lambda z: c_s.at[3, z, :, q], lambda k: c_r.at[k, 3, :, q])

    for r in square_copies:
        r.came()
    for r in sums:
        r.came()
    outs = []
    for a, device in ((1, to_xp), (2, to_yp), (3, to_diag), (0, None)):
        scale = lax.rsqrt(s_g[a][0:1, :] * (1.0 / WIDTH) + NORM_EPSILON)
        for p in range(4):
            v = c_s[p, zh, a].astype(F32)
            for k in range(3):
                v += c_r[k, p, a].astype(F32)
            gate = v[:, :8] * scale
            up = v[:, 8:] * scale
            hidden = (gate / (1.0 + jnp.exp(-gate)) * up).reshape(16, ROWS).astype(BF16)
            if device is None:
                h_r[0, p * 16:(p + 1) * 16, :] = hidden
            else:
                h_s[a - 1, p * 16:(p + 1) * 16, :] = hidden
        if device is not None:
            outs.append(remote(h_s.at[a - 1], h_r.at[a], device))

    u = lax.broadcasted_iota(jnp.int32, (256, 256), 0)
    col = lax.broadcasted_iota(jnp.int32, (256, 256), 1)
    slot, pair, zbit = u // 64, (u // 16) % 4, (u // 8) % 2
    xs = jnp.where(slot % 2 == 1, xp, x)
    ys = jnp.where(slot // 2 == 1, yp, y)
    xs = jnp.where(pair % 2 == 1, (xs + 3 + 2 * (xs % 2)) % 4, xs)
    ys = jnp.where(pair // 2 == 1, (ys + 3 + 2 * (ys % 2)) % 4, ys)
    zs = jnp.where(zbit == 1, 1 - zl, zl)
    shard = xs * 8 + zs * 4 + ys
    spread = (lax.broadcasted_iota(jnp.int32, (32, 256), 0)
              == lax.broadcasted_iota(jnp.int32, (32, 256), 1) // 8).astype(F32).astype(BF16)
    table = jnp.broadcast_to(table_ref[...].astype(F32), (8, 32)).astype(BF16)
    wanted = jnp.dot(table, spread, preferred_element_type=F32)[0:1, :].astype(jnp.int32)
    pick = jnp.where((shard == wanted) & (u % 8 == col % 8), 1.0, 0.0).astype(BF16)
    for r in outs:
        r.came()
    act_ref[...] = lax.dot_general(
        h_r[...].reshape(256, ROWS), pick, (((0,), (0,)), ((), ())), preferred_element_type=F32).astype(BF16)

    for r in used:
        r.sent()
    assert len(used) <= N_COPIES, len(used)


def gather_and_project(gradient, master, first_moment, second_moment, residual, norm_gain, shard_table, clip_limit):
    hbm = pl.BlockSpec(memory_space=pl.ANY)
    vmem = pl.BlockSpec(memory_space=pltpu.VMEM)
    slab = gradient.shape

    def kernel(*refs):
        step_kernel(clip_limit, *refs)

    return pl.pallas_call(
        kernel,
        out_shape=(
            jax.ShapeDtypeStruct((ROWS, 256), BF16),
            jax.ShapeDtypeStruct((8, 128), F32),
        ),
        in_specs=[hbm] * 6 + [vmem],
        out_specs=(vmem, vmem),
        scratch_shapes=[
            pltpu.VMEM(slab, BF16),
            pltpu.VMEM(slab, F32),
            pltpu.VMEM(slab, F32),
            pltpu.VMEM(slab, F32),
            pltpu.VMEM(slab, F32),
            pltpu.VMEM((16, 128), F32),
            pltpu.VMEM((4, 2, ROWS, K_DEV), BF16),
            pltpu.VMEM((8, 2, UNITS, K_DEV), BF16),
            pltpu.VMEM((UNITS, K_DEV), BF16),
            pltpu.VMEM((4, 4, 4, 2, 16, ROWS), BF16),
            pltpu.VMEM((3, 4, 4, 2, 16, ROWS), BF16),
            pltpu.VMEM((3, UNITS, ROWS), BF16),
            pltpu.VMEM((4, UNITS, ROWS), BF16),
            pltpu.VMEM((8, 128), F32),
            pltpu.VMEM((31, 8, 128), F32),
            pltpu.VMEM((8, 384), F32),
            pltpu.VMEM((7, 8, 384), F32),
            pltpu.VMEM((4, 8, ROWS), F32),
            pltpu.SemaphoreType.DMA((6,)),
            pltpu.SemaphoreType.DMA((N_COPIES,)),
            pltpu.SemaphoreType.DMA((N_COPIES,)),
            pltpu.SemaphoreType.DMA((4,)),
        ],
        compiler_params=pltpu.CompilerParams(
            collective_id=0, has_side_effects=True, vmem_limit_bytes=48 << 20),
        cost_estimate=pl.CostEstimate(
            flops=2 * 512 * 1024 * 4096, bytes_accessed=8 << 20, transcendentals=1 << 20),
        name="gather_project",
    )(gradient, master, first_moment, second_moment, residual,
      norm_gain.reshape(128, 128), shard_table.reshape(1, 32))


def attend(queries, layer_cache, fresh_entries, lengths):
    row_count, head_count, head_width = queries.shape
    group_count = layer_cache.shape[2]
    per_group = head_count // group_count
    score_scale = 1.0 / math.sqrt(head_width)
    grouped = queries.reshape(row_count, group_count, per_group, head_width)
    cached_keys = layer_cache[:, 0]
    cached_values = layer_cache[:, 1]
    scores = (
        jnp.einsum("rghd,rgpd->rghp", grouped, cached_keys, preferred_element_type=jnp.float32)
        * score_scale
    )
    own_score = (
        jnp.einsum(
            "rghd,rgd->rgh", grouped, fresh_entries[:, 0], preferred_element_type=jnp.float32
        )
        * score_scale
    )
    positions = lax.broadcasted_iota(jnp.int32, (row_count, 1, 1, cached_keys.shape[2]), 3)
    in_range = positions < lengths[:, None, None, None]
    scores = jnp.where(in_range, scores, -jnp.inf)
    row_peak = jnp.maximum(jnp.max(scores, axis=3), own_score)
    cached_exp = jnp.exp(scores - row_peak[..., None])
    own_exp = jnp.exp(own_score - row_peak)
    denominator = jnp.sum(cached_exp, axis=3) + own_exp
    cached_prob = (cached_exp / denominator[..., None]).astype(jnp.bfloat16)
    own_prob = (own_exp / denominator).astype(jnp.bfloat16)
    combined = jnp.einsum(
        "rghp,rgpd->rghd", cached_prob, cached_values, preferred_element_type=jnp.float32
    )
    combined = (
        combined
        + own_prob[..., None].astype(jnp.float32)
        * fresh_entries[:, 1].astype(jnp.float32)[:, :, None, :]
    )
    return combined.reshape(row_count, head_count, head_width).astype(jnp.bfloat16)


def per_device(
    gradient,
    master,
    first_moment,
    second_moment,
    residual,
    norm_gain,
    queries,
    layer_cache,
    fresh_entries,
    lengths,
    shard_table,
):
    entry_count = gradient.size * lax.axis_size("dp") * lax.axis_size("tensor")
    activated, clip = gather_and_project(
        gradient, master, first_moment, second_moment, residual, norm_gain, shard_table,
        CLIP_LEVEL * math.sqrt(entry_count))
    clipped = gradient.astype(jnp.float32) * clip[0, 0]
    new_first = FIRST_DECAY * first_moment + (1.0 - FIRST_DECAY) * clipped
    new_second = SECOND_DECAY * second_moment + (1.0 - SECOND_DECAY) * clipped * clipped
    attended = attend(queries, layer_cache, fresh_entries, lengths)
    return (new_first, new_second, attended, activated)


def solution(mesh):
    return jax.shard_map(
        per_device,
        mesh=mesh,
        in_specs=(
            P(None, "dp", "tensor"),
            P(None, "dp", "tensor"),
            P(None, "dp", "tensor"),
            P(None, "dp", "tensor"),
            P("dp", "tensor"),
            P(),
            P("dp", "tensor", None),
            P("dp", None, "tensor", None, None),
            P("dp", None, "tensor", None),
            P("dp"),
            P(),
        ),
        out_specs=(
            P(None, "dp", "tensor"),
            P(None, "dp", "tensor"),
            P("dp", "tensor", None),
            P("dp", "tensor"),
        ),
        check_vma=False,
    )
```

```python
import math

import jax
import jax.numpy as jnp
from jax import lax
from jax.experimental import pallas as pl
from jax.experimental.pallas import tpu as pltpu
from jax.sharding import PartitionSpec as P

LEARN_RATE = 0.001
CLIP_LEVEL = 0.5
CLIP_EPSILON = 1e-06
FIRST_DECAY = 0.9
SECOND_DECAY = 0.95
FIRST_CORRECTION = 1.0 - 0.9**10
SECOND_CORRECTION = 1.0 - 0.95**10
ADAM_EPSILON = 1e-08
NORM_EPSILON = 1e-05
SCORE_SCALE = 1.0 / math.sqrt(128)

MESH = pl.DeviceIdType.MESH
F32 = jnp.float32
BF16 = jnp.bfloat16

K_DEV = 2048
ROWS = 256
UNITS = 64
WIDTH = 16384


class Remote:
    def __init__(self, src, dst, sends, recvs, slot, device, arrives=None):
        self.copy = pltpu.make_async_remote_copy(
            src_ref=src, dst_ref=dst, send_sem=sends.at[slot], recv_sem=recvs.at[slot],
            device_id=device, device_id_type=MESH)
        arrives = dst if arrives is None else arrives
        self.inbound = pltpu.make_async_remote_copy(
            src_ref=arrives, dst_ref=arrives, send_sem=sends.at[slot], recv_sem=recvs.at[slot],
            device_id=device, device_id_type=MESH)
        self.copy.start()

    def sent(self):
        self.copy.wait_send()

    def came(self):
        self.inbound.wait_recv()


N_COPIES = 56


def step_kernel(
    clip_limit,
    grad_h, master_h, first_h, second_h, resid_h, gain_h, query_h, cache_h, fresh_h, length_ref, table_ref,
    first_o, second_o, attended_o, act_ref,
    g_v, ma_v, m_v, v_v, gf, gain_v, a_v, b_v, b_swap, c_s, c_r, h_s, h_r,
    p_s, p_r, t_s, t_r, s_g, q_v, kv_v, f_v, o_v, len_v, load_sem, sends, recvs, many,
):
    d = lax.axis_index("dp")
    t = lax.axis_index("tensor")
    x, zl, y = d // 8, (d // 4) % 2, d % 4
    zh, c = t // 2, t % 2
    oc = 1 - c
    xp, xq = x + 1 - 2 * (x % 2), (x + 3 + 2 * (x % 2)) % 4
    yp, yq = y + 1 - 2 * (y % 2), (y + 3 + 2 * (y % 2)) % 4

    def at(x_, zl_, y_, zh_=None, c_=None):
        zh_ = zh if zh_ is None else zh_
        c_ = c if c_ is None else c_
        return {"dp": x_ * 8 + zl_ * 4 + y_, "tensor": zh_ * 2 + c_}

    to_xp, to_yp, to_diag = at(xp, zl, y), at(x, zl, yp), at(xp, zl, yp)
    to_xq, to_yq, to_zl = at(xq, zl, y), at(x, zl, yq), at(x, 1 - zl, y)
    to_core = at(x, zl, y, zh, oc)

    barrier = pltpu.get_barrier_semaphore()
    for k in range(1, 8):
        pl.semaphore_signal(barrier, inc=1, device_id={"dp": d, "tensor": (t + k) % 8}, device_id_type=MESH)
    for k in range(1, 32):
        pl.semaphore_signal(barrier, inc=1, device_id={"dp": (d + k) % 32, "tensor": t}, device_id_type=MESH)

    loads = [
        pltpu.make_async_copy(grad_h, g_v, load_sem.at[0]),
        pltpu.make_async_copy(resid_h, a_v.at[0, c], load_sem.at[1]),
        pltpu.make_async_copy(gain_h.at[pl.ds(pl.multiple_of(t * 16, 16), 16)], gain_v, load_sem.at[2]),
        pltpu.make_async_copy(master_h, ma_v, load_sem.at[3]),
        pltpu.make_async_copy(first_h, m_v, load_sem.at[4]),
        pltpu.make_async_copy(second_h, v_v, load_sem.at[5]),
        pltpu.make_async_copy(query_h, q_v, load_sem.at[6]),
        pltpu.make_async_copy(fresh_h, f_v, load_sem.at[7]),
        pltpu.make_async_copy(cache_h, kv_v, load_sem.at[8]),
    ]
    for load in loads:
        load.start()

    used = []

    def remote(src, dst, device, arrives=None):
        r = Remote(src, dst, sends, recvs, len(used), device, arrives)
        used.append(r)
        return r

    loads[0].wait()

    def square(i, acc):
        g = g_v[i // 4, pl.ds(pl.multiple_of((i % 4) * 16, 16), 16), :].astype(F32)
        gf[i // 4, pl.ds(pl.multiple_of((i % 4) * 16, 16), 16), :] = g
        sq = g * g
        return acc + (sq[:8] + sq[8:])

    acc = lax.fori_loop(0, 8, square, jnp.zeros((8, K_DEV), F32))
    local = jnp.sum(jnp.sum(acc, axis=0, keepdims=True), axis=1, keepdims=True)
    p_s[...] = jnp.broadcast_to(local, (8, 128))

    pl.semaphore_wait(barrier, 38)

    for k in range(1, 32):
        pltpu.make_async_remote_copy(
            src_ref=p_s, dst_ref=p_r.at[k - 1], send_sem=many.at[0], recv_sem=many.at[1],
            device_id={"dp": (d + k) % 32, "tensor": t}, device_id_type=MESH).start()

    loads[1].wait()
    ones = jnp.ones((8, 512), BF16)
    row_squares = jnp.zeros((8, ROWS), F32)
    for k in range(4):
        r = a_v[0, c, :, k * 512:(k + 1) * 512].astype(F32)
        sq = r * r
        high = sq.astype(BF16)
        low = (sq - high.astype(F32)).astype(BF16)
        for part in (high, low):
            row_squares += lax.dot_general(ones, part, (((1,), (1,)), ((), ())), preferred_element_type=F32)

    t_s[:, 128:] = row_squares

    row8 = lax.broadcasted_iota(jnp.int32, (32, ROWS), 1)
    spread_len = jnp.where(
        lax.broadcasted_iota(jnp.int32, (ROWS, 256), 0) % 8
        == lax.broadcasted_iota(jnp.int32, (ROWS, 256), 1) // 32, 1.0, 0.0).astype(BF16)
    own_len = jnp.where(
        row8 // 8 == lax.broadcasted_iota(jnp.int32, (32, ROWS), 0),
        jnp.broadcast_to(length_ref[...].astype(F32), (32, ROWS)), 0.0).astype(BF16)
    len_v[...] = jnp.dot(own_len, spread_len, preferred_element_type=F32)
    for load in loads[6:]:
        load.wait()

    def attend_block(g):
        rows = pl.ds(pl.multiple_of(g * 8, 8), 8)
        q = q_v[rows].reshape(128, 128)
        keys = kv_v[rows, 0].reshape(256, 128)
        values = kv_v[rows, 1].reshape(256, 128)
        own = f_v[rows, :]
        own_key = jnp.broadcast_to(own[:, :128].reshape(8, 1, 128), (8, 16, 128)).reshape(128, 128)
        own_value = jnp.broadcast_to(own[:, 128:].reshape(8, 1, 128), (8, 16, 128)).reshape(128, 128)
        head = lax.broadcasted_iota(jnp.int32, (128, 256), 0)
        pos = lax.broadcasted_iota(jnp.int32, (128, 256), 1)
        scores = lax.dot_general(q, keys, (((1,), (1,)), ((), ())), preferred_element_type=F32) * SCORE_SCALE
        own_score = jnp.sum(q.astype(F32) * own_key, axis=1, keepdims=True) * SCORE_SCALE
        valid = (head // 16 == pos // 32) & ((pos % 32).astype(F32) < len_v[pl.ds(g, 1), :])
        scores = jnp.where(valid, scores, -jnp.inf)
        peak = jnp.maximum(jnp.max(scores, axis=1, keepdims=True), own_score)
        cached = jnp.exp(scores - peak)
        fresh_exp = jnp.exp(own_score - peak)
        inverse = 1.0 / (jnp.sum(cached, axis=1, keepdims=True) + fresh_exp)
        prob = (cached * inverse).astype(BF16)
        own_prob = (fresh_exp * inverse).astype(BF16).astype(F32)
        out = jnp.dot(prob, values, preferred_element_type=F32) + own_prob * own_value
        o_v[rows] = out.astype(BF16).reshape(8, 16, 128)

    def attend(first, last):
        @pl.loop(first, last)
        def _(g):
            attend_block(g)

    attend(0, 8)

    everyone = pltpu.make_async_remote_copy(
        src_ref=p_r, dst_ref=p_r, send_sem=many.at[0], recv_sem=many.at[1],
        device_id=to_core, device_id_type=MESH)
    everyone.wait_send()
    everyone.wait_recv()
    total = p_s[...]
    for k in range(31):
        total += p_r[k]
    t_s[:, :128] = total

    for k in range(1, 8):
        pltpu.make_async_remote_copy(
            src_ref=t_s, dst_ref=t_r.at[k - 1], send_sem=many.at[2], recv_sem=many.at[3],
            device_id={"dp": d, "tensor": (t + k) % 8}, device_id_type=MESH).start()

    def rows_of(slot, half, r):
        return a_v.at[slot, half, pl.ds(r * 128, 128)]

    def to_other_core(slot, r):
        return remote(rows_of(slot, c, r), rows_of(slot, c, r), to_core, rows_of(slot, oc, r))

    rows_x = [remote(rows_of(0, c, r), rows_of(1, c, r), to_xp) for r in range(2)]
    rows_y = [remote(rows_of(0, c, r), rows_of(2, c, r), to_yp) for r in range(2)]
    core_rows = [to_other_core(0, 0), to_other_core(0, 1)]

    attend(8, 18)

    team = pltpu.make_async_remote_copy(
        src_ref=t_r, dst_ref=t_r, send_sem=many.at[2], recv_sem=many.at[3],
        device_id=to_core, device_id_type=MESH)
    team.wait_send()
    team.wait_recv()
    both = t_s[...]
    for k in range(7):
        both += t_r[k]
    clip = jnp.minimum(1.0, clip_limit / (jnp.sqrt(both[:, :128]) + CLIP_EPSILON))
    s_g[0] = both[:, 128:]
    square_copies = [remote(s_g.at[0], s_g.at[slot], device) for slot, device in ((1, to_xp), (2, to_yp), (3, to_diag))]

    for load in loads[2:6]:
        load.wait()
    clip_one = clip[0:1, 0:1]
    gain = jnp.concatenate([gain_v[i:i + 1, :] for i in range(16)], axis=1)

    def fresh(parity, zone):
        row = pl.multiple_of((2 * zone + parity) * 8, 8)
        parts = []
        for i in range(2):
            clipped = gf[i, pl.ds(row, 8), :] * clip_one
            new_first = FIRST_DECAY * m_v[i, pl.ds(row, 8), :] + (1.0 - FIRST_DECAY) * clipped
            new_second = SECOND_DECAY * v_v[i, pl.ds(row, 8), :] + (1.0 - SECOND_DECAY) * clipped * clipped
            step = (new_first * (LEARN_RATE / FIRST_CORRECTION)) / (
                jnp.sqrt(new_second * (1.0 / SECOND_CORRECTION)) + ADAM_EPSILON)
            m_v[i, pl.ds(row, 8), :] = new_first
            v_v[i, pl.ds(row, 8), :] = new_second
            parts.append((ma_v[i, pl.ds(row, 8), :] - step) * gain)
        return jnp.concatenate(parts, axis=0).astype(BF16)

    @pl.loop(0, 4)
    def _(zone):
        b_swap[pl.ds(pl.multiple_of(zone * 16, 16), 16), :] = fresh(oc, zone)

    swap = remote(b_swap, b_v.at[0, c], to_core, b_v.at[0, oc])

    @pl.loop(0, 4)
    def _(zone):
        b_v[0, c, pl.ds(pl.multiple_of(zone * 16, 16), 16), :] = fresh(c, zone)

    def piece(slot, k):
        return b_v.at[slot, c if k == 0 else oc]

    def units(src, dst, k, device):
        return remote(piece(src, k), piece(dst, k), device)

    unit = {}
    for k in range(2):
        if k == 1:
            swap.came()
        unit[1, k] = units(0, 1, k, to_zl)
        unit[2, k] = units(0, 2, k, to_xq)
        unit[4, k] = units(0, 4, k, to_yq)

    stores = [
        pltpu.make_async_copy(m_v, first_o, load_sem.at[9]),
        pltpu.make_async_copy(v_v, second_o, load_sem.at[10]),
        pltpu.make_async_copy(o_v, attended_o, load_sem.at[11]),
    ]
    stores[0].start()
    stores[1].start()
    attend(18, 32)
    stores[2].start()

    core_got = []
    diag = []

    def pass_rows(r):
        rows_x[r].came()
        core_got.append(to_other_core(1, r))
        if r == 0:
            diag.append(remote(rows_of(1, c, 0), rows_of(3, c, 0), to_yp))
        rows_y[r].came()
        core_got.append(to_other_core(2, r))
        if r == 1:
            diag.append(remote(rows_of(2, c, 1), rows_of(3, c, 1), to_xp))

    pass_rows(0)
    for k in range(2):
        unit[1, k].came()
        unit[3, k] = units(1, 3, k, to_xq)
        unit[5, k] = units(1, 5, k, to_yq)
    unit[2, 0].came()
    unit[6, 0] = units(2, 6, 0, to_yq)
    unit[4, 0].came()
    unit[4, 1].came()
    unit[6, 1] = units(4, 6, 1, to_xq)
    unit[2, 1].came()
    pass_rows(1)
    for r in core_rows + core_got:
        r.came()

    def product(slot, count, a):
        out = jnp.zeros((count * UNITS, ROWS), F32)
        for h in range(2):
            lhs = b_v[slot:slot + count, h].reshape(count * UNITS, K_DEV)
            out += lax.dot_general(lhs, a_v[a, h], (((1,), (1,)), ((), ())), preferred_element_type=F32)
        return out.reshape(count, 4, 16, ROWS).astype(BF16)

    def pair_tile(p, a):
        out = product(2 * p, 2, a)
        for z in range(4):
            c_s[p, z, a] = out[:, z]

    sums = []

    def send_sums(view_s, view_r):
        for k in range(1, 4):
            z = (zh + k) % 4
            sums.append(remote(view_s(z), view_r(k - 1), at(x, zl, y, z, c)))

    def pair_three(p):
        @pl.loop(0, 3)
        def _(a):
            pair_tile(p, a)

        send_sums(lambda z: c_s.at[p, z, pl.ds(0, 3)], lambda k: c_r.at[k, p, pl.ds(0, 3)])

    pair_three(0)
    unit[3, 0].came()
    unit[7, 0] = units(3, 7, 0, to_yq)
    unit[5, 0].came()
    unit[5, 1].came()
    unit[7, 1] = units(5, 7, 1, to_xq)
    unit[3, 1].came()
    pair_three(1)
    pair_three(2)
    last_rows = []
    for r in range(2):
        diag[r].came()
        last_rows.append(to_other_core(3, r))
    for r in last_rows:
        r.came()
    for p in range(3):
        pair_tile(p, 3)
    send_sums(lambda z: c_s.at[pl.ds(0, 3), z, 3], lambda k: c_r.at[k, pl.ds(0, 3), 3])

    for q in range(2):
        for k in range(2):
            unit[6 + q, k].came()

        @pl.loop(0, 4)
        def _(a):
            out = product(6 + q, 1, a)
            for z in range(4):
                c_s[3, z, a, q] = out[0, z]

        send_sums(lambda z: c_s.at[3, z, :, q], lambda k: c_r.at[k, 3, :, q])

    for r in square_copies:
        r.came()
    for r in sums:
        r.came()
    outs = []
    for a, device in ((1, to_xp), (2, to_yp), (3, to_diag), (0, None)):
        scale = lax.rsqrt(s_g[a][0:1, :] * (1.0 / WIDTH) + NORM_EPSILON)
        for p in range(4):
            v = c_s[p, zh, a].astype(F32)
            for k in range(3):
                v += c_r[k, p, a].astype(F32)
            gate = v[:, :8] * scale
            up = v[:, 8:] * scale
            hidden = (gate / (1.0 + jnp.exp(-gate)) * up).reshape(16, ROWS).astype(BF16)
            if device is None:
                h_r[0, p * 16:(p + 1) * 16, :] = hidden
            else:
                h_s[a - 1, p * 16:(p + 1) * 16, :] = hidden
        if device is not None:
            outs.append(remote(h_s.at[a - 1], h_r.at[a], device))

    u = lax.broadcasted_iota(jnp.int32, (256, 256), 0)
    col = lax.broadcasted_iota(jnp.int32, (256, 256), 1)
    slot, pair, zbit = u // 64, (u // 16) % 4, (u // 8) % 2
    xs = jnp.where(slot % 2 == 1, xp, x)
    ys = jnp.where(slot // 2 == 1, yp, y)
    xs = jnp.where(pair % 2 == 1, (xs + 3 + 2 * (xs % 2)) % 4, xs)
    ys = jnp.where(pair // 2 == 1, (ys + 3 + 2 * (ys % 2)) % 4, ys)
    zs = jnp.where(zbit == 1, 1 - zl, zl)
    shard = xs * 8 + zs * 4 + ys
    spread = (lax.broadcasted_iota(jnp.int32, (32, 256), 0)
              == lax.broadcasted_iota(jnp.int32, (32, 256), 1) // 8).astype(F32).astype(BF16)
    table = jnp.broadcast_to(table_ref[...].astype(F32), (8, 32)).astype(BF16)
    wanted = jnp.dot(table, spread, preferred_element_type=F32)[0:1, :].astype(jnp.int32)
    pick = jnp.where((shard == wanted) & (u % 8 == col % 8), 1.0, 0.0).astype(BF16)
    for r in outs:
        r.came()
    act_ref[...] = lax.dot_general(
        h_r[...].reshape(256, ROWS), pick, (((0,), (0,)), ((), ())), preferred_element_type=F32).astype(BF16)

    for store in stores:
        store.wait()
    for r in used:
        r.sent()
    assert len(used) <= N_COPIES, len(used)


def step(gradient, master, first_moment, second_moment, residual, norm_gain,
         queries, layer_cache, fresh_entries, lengths, shard_table, clip_limit):
    hbm = pl.BlockSpec(memory_space=pl.ANY)
    vmem = pl.BlockSpec(memory_space=pltpu.VMEM)
    slab = gradient.shape

    def kernel(*refs):
        step_kernel(clip_limit, *refs)

    return pl.pallas_call(
        kernel,
        out_shape=(
            jax.ShapeDtypeStruct(slab, F32),
            jax.ShapeDtypeStruct(slab, F32),
            jax.ShapeDtypeStruct(queries.shape, BF16),
            jax.ShapeDtypeStruct((ROWS, 256), BF16),
        ),
        in_specs=[hbm] * 9 + [vmem] * 2,
        out_specs=(hbm, hbm, hbm, vmem),
        scratch_shapes=[
            pltpu.VMEM(slab, BF16),
            pltpu.VMEM(slab, F32),
            pltpu.VMEM(slab, F32),
            pltpu.VMEM(slab, F32),
            pltpu.VMEM(slab, F32),
            pltpu.VMEM((16, 128), F32),
            pltpu.VMEM((4, 2, ROWS, K_DEV), BF16),
            pltpu.VMEM((8, 2, UNITS, K_DEV), BF16),
            pltpu.VMEM((UNITS, K_DEV), BF16),
            pltpu.VMEM((4, 4, 4, 2, 16, ROWS), BF16),
            pltpu.VMEM((3, 4, 4, 2, 16, ROWS), BF16),
            pltpu.VMEM((3, UNITS, ROWS), BF16),
            pltpu.VMEM((4, UNITS, ROWS), BF16),
            pltpu.VMEM((8, 128), F32),
            pltpu.VMEM((31, 8, 128), F32),
            pltpu.VMEM((8, 384), F32),
            pltpu.VMEM((7, 8, 384), F32),
            pltpu.VMEM((4, 8, ROWS), F32),
            pltpu.VMEM(queries.shape, BF16),
            pltpu.VMEM((ROWS, 2, 32, 128), BF16),
            pltpu.VMEM((ROWS, 256), F32),
            pltpu.VMEM(queries.shape, BF16),
            pltpu.VMEM((32, 256), F32),
            pltpu.SemaphoreType.DMA((12,)),
            pltpu.SemaphoreType.DMA((N_COPIES,)),
            pltpu.SemaphoreType.DMA((N_COPIES,)),
            pltpu.SemaphoreType.DMA((4,)),
        ],
        compiler_params=pltpu.CompilerParams(
            collective_id=0, has_side_effects=True, vmem_limit_bytes=56 << 20),
        name="step",
    )(gradient, master, first_moment, second_moment, residual,
      norm_gain.reshape(128, 128), queries, layer_cache.reshape(ROWS, 2, 32, 128),
      fresh_entries.astype(F32).reshape(ROWS, 256), lengths.reshape(1, ROWS), shard_table.reshape(1, 32))


def per_device(gradient, master, first_moment, second_moment, residual, norm_gain,
               queries, layer_cache, fresh_entries, lengths, shard_table):
    entry_count = gradient.size * lax.axis_size("dp") * lax.axis_size("tensor")
    return step(
        gradient, master, first_moment, second_moment, residual, norm_gain,
        queries, layer_cache, fresh_entries, lengths, shard_table,
        CLIP_LEVEL * math.sqrt(entry_count))


def solution(mesh):
    return jax.shard_map(
        per_device,
        mesh=mesh,
        in_specs=(
            P(None, "dp", "tensor"),
            P(None, "dp", "tensor"),
            P(None, "dp", "tensor"),
            P(None, "dp", "tensor"),
            P("dp", "tensor"),
            P(),
            P("dp", "tensor", None),
            P("dp", None, "tensor", None, None),
            P("dp", None, "tensor", None),
            P("dp"),
            P(),
        ),
        out_specs=(
            P(None, "dp", "tensor"),
            P(None, "dp", "tensor"),
            P("dp", "tensor", None),
            P("dp", "tensor"),
        ),
        check_vma=False,
    )
```

```python
import math

import jax
import jax.numpy as jnp
from jax import lax
from jax.experimental import pallas as pl
from jax.experimental.pallas import tpu as pltpu
from jax.sharding import PartitionSpec as P

LEARN_RATE = 0.001
CLIP_LEVEL = 0.5
CLIP_EPSILON = 1e-06
FIRST_DECAY = 0.9
SECOND_DECAY = 0.95
FIRST_CORRECTION = 1.0 - 0.9**10
SECOND_CORRECTION = 1.0 - 0.95**10
ADAM_EPSILON = 1e-08
NORM_EPSILON = 1e-05
SCORE_SCALE = 1.0 / math.sqrt(128)

MESH = pl.DeviceIdType.MESH
F32 = jnp.float32
BF16 = jnp.bfloat16

K_DEV = 2048
ROWS = 256
UNITS = 64
WIDTH = 16384


class Remote:
    def __init__(self, src, dst, sends, recvs, slot, device, arrives=None):
        self.copy = pltpu.make_async_remote_copy(
            src_ref=src, dst_ref=dst, send_sem=sends.at[slot], recv_sem=recvs.at[slot],
            device_id=device, device_id_type=MESH)
        arrives = dst if arrives is None else arrives
        self.inbound = pltpu.make_async_remote_copy(
            src_ref=arrives, dst_ref=arrives, send_sem=sends.at[slot], recv_sem=recvs.at[slot],
            device_id=device, device_id_type=MESH)
        self.copy.start()

    def sent(self):
        self.copy.wait_send()

    def came(self):
        self.inbound.wait_recv()


N_COPIES = 56


def step_kernel(
    clip_limit,
    grad_h, master_h, first_h, second_h, resid_h, gain_h, query_h, cache_h, fresh_h, length_ref, table_ref,
    first_o, second_o, attended_o, act_ref,
    g_v, ma_v, m_v, v_v, gf, gain_v, a_v, b_v, b_swap, c_s, c_r, h_s, h_r,
    p_s, p_r, t_s, t_r, s_g, q_v, kv_v, f_v, o_v, len_v, last, load_sem, sends, recvs, many,
):
    d = lax.axis_index("dp")
    t = lax.axis_index("tensor")
    x, zl, y = d // 8, (d // 4) % 2, d % 4
    zh, c = t // 2, t % 2
    oc = 1 - c
    xp, xq = x + 1 - 2 * (x % 2), (x + 3 + 2 * (x % 2)) % 4
    yp, yq = y + 1 - 2 * (y % 2), (y + 3 + 2 * (y % 2)) % 4

    def at(x_, zl_, y_, zh_=None, c_=None):
        zh_ = zh if zh_ is None else zh_
        c_ = c if c_ is None else c_
        return {"dp": x_ * 8 + zl_ * 4 + y_, "tensor": zh_ * 2 + c_}

    to_xp, to_yp, to_diag = at(xp, zl, y), at(x, zl, yp), at(xp, zl, yp)
    to_xq, to_yq, to_zl = at(xq, zl, y), at(x, zl, yq), at(x, 1 - zl, y)
    to_core = at(x, zl, y, zh, oc)

    near = [
        at(x_, z_, y_, zh, c_)
        for x_ in (x, xp) for y_ in (y, yp) for z_ in (zl, 1 - zl) for c_ in (c, oc)
    ][1:]
    far = [
        at(x_, 1 - zl if k == 2 else zl, y_, (zh + k) % 4, c)
        for x_ in (x, xq) for y_ in (y, yq) for k in range(4)
    ][1:]
    team = [at(x, zl, y, (zh + k // 2) % 4, (c + k) % 2) for k in range(1, 8)]

    loads = [
        pltpu.make_async_copy(grad_h, g_v, load_sem.at[0]),
        pltpu.make_async_copy(resid_h, a_v.at[0, c], load_sem.at[1]),
        pltpu.make_async_copy(gain_h.at[pl.ds(pl.multiple_of(t * 16, 16), 16)], gain_v, load_sem.at[2]),
        pltpu.make_async_copy(master_h, ma_v, load_sem.at[3]),
        pltpu.make_async_copy(first_h, m_v, load_sem.at[4]),
        pltpu.make_async_copy(second_h, v_v, load_sem.at[5]),
        pltpu.make_async_copy(query_h, q_v, load_sem.at[6]),
        pltpu.make_async_copy(fresh_h, f_v, load_sem.at[7]),
        pltpu.make_async_copy(cache_h, kv_v, load_sem.at[8]),
    ]
    loads[0].start()
    barrier = pltpu.get_barrier_semaphore()
    greeted = near + far + [team[k] for k in (2, 3, 4, 6)]
    for peer in greeted:
        pl.semaphore_signal(barrier, inc=1, device_id=peer, device_id_type=MESH)

    used = []

    def remote(src, dst, device, arrives=None):
        r = Remote(src, dst, sends, recvs, len(used), device, arrives)
        used.append(r)
        return r

    loads[0].wait()
    for load in loads[1:]:
        load.start()

    def square(i, acc):
        g = g_v[i // 4, pl.ds(pl.multiple_of((i % 4) * 16, 16), 16), :].astype(F32)
        gf[i // 4, pl.ds(pl.multiple_of((i % 4) * 16, 16), 16), :] = g
        sq = g * g
        return acc + (sq[:8] + sq[8:])

    acc = lax.fori_loop(0, 8, square, jnp.zeros((8, K_DEV), F32))
    local = jnp.sum(jnp.sum(acc, axis=0, keepdims=True), axis=1, keepdims=True)
    p_s[0] = jnp.broadcast_to(local, (8, 128))

    pl.semaphore_wait(barrier, len(greeted))

    def to_all(src, dst, peers, pair):
        for k, peer in enumerate(peers):
            pltpu.make_async_remote_copy(
                src_ref=src, dst_ref=dst.at[k], send_sem=many.at[pair], recv_sem=many.at[pair + 1],
                device_id=peer, device_id_type=MESH).start()

    def from_all(dst, pair):
        whole = pltpu.make_async_remote_copy(
            src_ref=dst, dst_ref=dst, send_sem=many.at[pair], recv_sem=many.at[pair + 1],
            device_id=to_core, device_id_type=MESH)
        whole.wait_send()
        whole.wait_recv()

    to_all(p_s.at[0], p_r.at[0], near, 0)

    loads[1].wait()
    ones = jnp.ones((8, 512), BF16)
    row_squares = jnp.zeros((8, ROWS), F32)
    for k in range(4):
        r = a_v[0, c, :, k * 512:(k + 1) * 512].astype(F32)
        sq = r * r
        high = sq.astype(BF16)
        low = (sq - high.astype(F32)).astype(BF16)
        for part in (high, low):
            row_squares += lax.dot_general(ones, part, (((1,), (1,)), ((), ())), preferred_element_type=F32)

    t_s[...] = row_squares

    row8 = lax.broadcasted_iota(jnp.int32, (32, ROWS), 1)
    spread_len = jnp.where(
        lax.broadcasted_iota(jnp.int32, (ROWS, 256), 0) % 8
        == lax.broadcasted_iota(jnp.int32, (ROWS, 256), 1) // 32, 1.0, 0.0).astype(BF16)
    own_len = jnp.where(
        row8 // 8 == lax.broadcasted_iota(jnp.int32, (32, ROWS), 0),
        jnp.broadcast_to(length_ref[...].astype(F32), (32, ROWS)), 0.0).astype(BF16)
    len_v[...] = jnp.dot(own_len, spread_len, preferred_element_type=F32)
    for load in loads[6:]:
        load.wait()

    def attend_block(g):
        rows = pl.ds(pl.multiple_of(g * 8, 8), 8)
        q = q_v[rows].reshape(128, 128)
        keys = kv_v[rows, 0].reshape(256, 128)
        values = kv_v[rows, 1].reshape(256, 128)
        own_key = jnp.broadcast_to(f_v[rows, 0].astype(F32), (8, 16, 128)).reshape(128, 128)
        own_value = jnp.broadcast_to(f_v[rows, 1].astype(F32), (8, 16, 128)).reshape(128, 128)
        head = lax.broadcasted_iota(jnp.int32, (128, 256), 0)
        pos = lax.broadcasted_iota(jnp.int32, (128, 256), 1)
        scores = lax.dot_general(q, keys, (((1,), (1,)), ((), ())), preferred_element_type=F32) * SCORE_SCALE
        own_score = jnp.sum(q.astype(F32) * own_key, axis=1, keepdims=True) * SCORE_SCALE
        valid = (head // 16 == pos // 32) & ((pos % 32).astype(F32) < len_v[pl.ds(g, 1), :])
        scores = jnp.where(valid, scores, -jnp.inf)
        peak = jnp.maximum(jnp.max(scores, axis=1, keepdims=True), own_score)
        cached = jnp.exp(scores - peak)
        fresh_exp = jnp.exp(own_score - peak)
        inverse = 1.0 / (jnp.sum(cached, axis=1, keepdims=True) + fresh_exp)
        prob = (cached * inverse).astype(BF16)
        own_prob = (fresh_exp * inverse).astype(BF16).astype(F32)
        out = jnp.dot(prob, values, preferred_element_type=F32) + own_prob * own_value
        o_v[rows] = out.astype(BF16).reshape(8, 16, 128)

    def attend(first, last):
        @pl.loop(first, last)
        def _(g):
            attend_block(g)

    from_all(p_r.at[0], 0)
    total = p_s[0]
    for k in range(15):
        total += p_r[0, k]
    p_s[1] = total
    to_all(p_s.at[1], p_r.at[1], far, 2)
    to_all(t_s, t_r, team, 4)

    def rows_of(slot, half, r):
        return a_v.at[slot, half, pl.ds(r * 128, 128)]

    def to_other_core(slot, r):
        return remote(rows_of(slot, c, r), rows_of(slot, c, r), to_core, rows_of(slot, oc, r))

    rows_x = [remote(rows_of(0, c, r), rows_of(1, c, r), to_xp) for r in range(2)]
    rows_y = [remote(rows_of(0, c, r), rows_of(2, c, r), to_yp) for r in range(2)]
    core_rows = [to_other_core(0, 0), to_other_core(0, 1)]

    attend(0, 10)

    from_all(p_r.at[1], 2)
    total = p_s[1]
    for k in range(15):
        total += p_r[1, k]
    clip = jnp.minimum(1.0, clip_limit / (jnp.sqrt(total) + CLIP_EPSILON))

    for load in loads[2:6]:
        load.wait()
    clip_one = clip[0:1, 0:1]
    gain = jnp.concatenate([gain_v[i:i + 1, :] for i in range(16)], axis=1)

    def fresh(parity, zone):
        row = pl.multiple_of((2 * zone + parity) * 8, 8)
        parts = []
        for i in range(2):
            clipped = gf[i, pl.ds(row, 8), :] * clip_one
            new_first = FIRST_DECAY * m_v[i, pl.ds(row, 8), :] + (1.0 - FIRST_DECAY) * clipped
            new_second = SECOND_DECAY * v_v[i, pl.ds(row, 8), :] + (1.0 - SECOND_DECAY) * clipped * clipped
            step = (new_first * (LEARN_RATE / FIRST_CORRECTION)) / (
                jnp.sqrt(new_second * (1.0 / SECOND_CORRECTION)) + ADAM_EPSILON)
            m_v[i, pl.ds(row, 8), :] = new_first
            v_v[i, pl.ds(row, 8), :] = new_second
            parts.append((ma_v[i, pl.ds(row, 8), :] - step) * gain)
        return jnp.concatenate(parts, axis=0).astype(BF16)

    @pl.loop(0, 4)
    def _(zone):
        b_swap[pl.ds(pl.multiple_of(zone * 16, 16), 16), :] = fresh(oc, zone)

    swap = remote(b_swap, b_v.at[0, c], to_core, b_v.at[0, oc])

    @pl.loop(0, 4)
    def _(zone):
        b_v[0, c, pl.ds(pl.multiple_of(zone * 16, 16), 16), :] = fresh(c, zone)

    def piece(slot, k):
        return b_v.at[slot, c if k == 0 else oc]

    def units(src, dst, k, device):
        return remote(piece(src, k), piece(dst, k), device)

    unit = {}
    for k in range(2):
        if k == 1:
            swap.came()
        unit[1, k] = units(0, 1, k, to_zl)
        unit[2, k] = units(0, 2, k, to_xq)
        unit[4, k] = units(0, 4, k, to_yq)

    stores = [
        pltpu.make_async_copy(m_v, first_o, load_sem.at[9]),
        pltpu.make_async_copy(v_v, second_o, load_sem.at[10]),
        pltpu.make_async_copy(o_v, attended_o, load_sem.at[11]),
    ]
    stores[0].start()
    stores[1].start()
    from_all(t_r, 4)
    squares = t_s[...]
    for k in range(7):
        squares += t_r[k]
    s_g[0] = squares
    square_copies = [remote(s_g.at[0], s_g.at[slot], device) for slot, device in ((1, to_xp), (2, to_yp), (3, to_diag))]
    attend(10, 32)
    stores[2].start()

    core_got = []
    diag = []

    def pass_rows(r):
        rows_x[r].came()
        core_got.append(to_other_core(1, r))
        if r == 0:
            diag.append(remote(rows_of(1, c, 0), rows_of(3, c, 0), to_yp))
        rows_y[r].came()
        core_got.append(to_other_core(2, r))
        if r == 1:
            diag.append(remote(rows_of(2, c, 1), rows_of(3, c, 1), to_xp))

    pass_rows(0)
    for k in range(2):
        unit[1, k].came()
        unit[3, k] = units(1, 3, k, to_xq)
        unit[5, k] = units(1, 5, k, to_yq)
    unit[2, 0].came()
    unit[6, 0] = units(2, 6, 0, to_yq)
    unit[4, 0].came()
    unit[4, 1].came()
    unit[6, 1] = units(4, 6, 1, to_xq)
    unit[2, 1].came()
    pass_rows(1)
    for r in core_rows + core_got:
        r.came()

    def half_product(slot, count, a, h):
        lhs = b_v[slot:slot + count, h].reshape(count * UNITS, K_DEV)
        return lax.dot_general(lhs, a_v[a, h], (((1,), (1,)), ((), ())), preferred_element_type=F32)

    def product(slot, count, a):
        out = half_product(slot, count, a, 0) + half_product(slot, count, a, 1)
        return out.reshape(count, 4, 16, ROWS).astype(BF16)

    def pair_tile(p, a):
        out = product(2 * p, 2, a)
        for z in range(4):
            c_s[p, z, a] = out[:, z]

    sums = []

    def send_sums(view_s, view_r):
        for k in range(1, 4):
            z = (zh + k) % 4
            sums.append(remote(view_s(z), view_r(k - 1), at(x, zl, y, z, c)))

    def pair_three(p):
        @pl.loop(0, 3)
        def _(a):
            pair_tile(p, a)

        send_sums(lambda z: c_s.at[p, z, pl.ds(0, 3)], lambda k: c_r.at[k, p, pl.ds(0, 3)])

    pair_three(0)
    unit[3, 0].came()
    unit[7, 0] = units(3, 7, 0, to_yq)
    unit[5, 0].came()
    unit[5, 1].came()
    unit[7, 1] = units(5, 7, 1, to_xq)
    unit[3, 1].came()
    pair_three(1)
    pair_three(2)
    last_rows = []
    for r in range(2):
        diag[r].came()
        last_rows.append(to_other_core(3, r))
    for r in last_rows:
        r.came()
    for p in range(3):
        pair_tile(p, 3)
    send_sums(lambda z: c_s.at[pl.ds(0, 3), z, 3], lambda k: c_r.at[k, pl.ds(0, 3), 3])

    for k in range(2):
        unit[6, k].came()

    @pl.loop(0, 4)
    def _(a):
        out = product(6, 1, a)
        for z in range(4):
            c_s[3, z, a, 0] = out[0, z]

    send_sums(lambda z: c_s.at[3, z, :, 0], lambda k: c_r.at[k, 3, :, 0])

    u = lax.broadcasted_iota(jnp.int32, (256, 256), 0)
    col = lax.broadcasted_iota(jnp.int32, (256, 256), 1)
    slot, pair, zbit = u // 64, (u // 16) % 4, (u // 8) % 2
    xs = jnp.where(slot % 2 == 1, xp, x)
    ys = jnp.where(slot // 2 == 1, yp, y)
    xs = jnp.where(pair % 2 == 1, (xs + 3 + 2 * (xs % 2)) % 4, xs)
    ys = jnp.where(pair // 2 == 1, (ys + 3 + 2 * (ys % 2)) % 4, ys)
    zs = jnp.where(zbit == 1, 1 - zl, zl)
    shard = xs * 8 + zs * 4 + ys
    spread = (lax.broadcasted_iota(jnp.int32, (32, 256), 0)
              == lax.broadcasted_iota(jnp.int32, (32, 256), 1) // 8).astype(F32).astype(BF16)
    table = jnp.broadcast_to(table_ref[...].astype(F32), (8, 32)).astype(BF16)
    wanted = jnp.dot(table, spread, preferred_element_type=F32)[0:1, :].astype(jnp.int32)
    pick = jnp.where((shard == wanted) & (u % 8 == col % 8), 1.0, 0.0).astype(BF16)
    unit[7, 0].came()

    @pl.loop(0, 4)
    def _(a):
        last[a] = half_product(7, 1, a, c)

    unit[7, 1].came()

    @pl.loop(0, 4)
    def _(a):
        out = (last[a] + half_product(7, 1, a, oc)).reshape(4, 16, ROWS).astype(BF16)
        for z in range(4):
            c_s[3, z, a, 1] = out[z]

    send_sums(lambda z: c_s.at[3, z, :, 1], lambda k: c_r.at[k, 3, :, 1])

    for r in square_copies:
        r.came()

    def activations(a, p):
        scale = lax.rsqrt(s_g[a][0:1, :] * (1.0 / WIDTH) + NORM_EPSILON)
        v = c_s[p, zh, a].astype(F32)
        for k in range(3):
            v += c_r[k, p, a].astype(F32)
        gate = v[:, :8] * scale
        up = v[:, 8:] * scale
        hidden = (gate / (1.0 + jnp.exp(-gate)) * up).reshape(16, ROWS).astype(BF16)
        h_s[a, p * 16:(p + 1) * 16, :] = hidden

    for r in sums[:12]:
        r.came()
    for a in range(4):
        for p in range(3):
            activations(a, p)
    for r in sums[12:]:
        r.came()
    outs = []
    for a, device in ((3, to_diag), (1, to_xp), (2, to_yp)):
        activations(a, 3)
        outs.append(remote(h_s.at[a], h_r.at[a], device))
    activations(0, 3)
    h_r[0] = h_s[0]
    for r in outs:
        r.came()
    act_ref[...] = lax.dot_general(
        h_r[...].reshape(256, ROWS), pick, (((0,), (0,)), ((), ())), preferred_element_type=F32).astype(BF16)

    for store in stores:
        store.wait()
    for r in used:
        r.sent()
    assert len(used) <= N_COPIES, len(used)


def step(gradient, master, first_moment, second_moment, residual, norm_gain,
         queries, layer_cache, fresh_entries, lengths, shard_table, clip_limit):
    hbm = pl.BlockSpec(memory_space=pl.ANY)
    vmem = pl.BlockSpec(memory_space=pltpu.VMEM)
    slab = gradient.shape

    def kernel(*refs):
        step_kernel(clip_limit, *refs)

    results = pl.pallas_call(
        kernel,
        out_shape=(
            jax.ShapeDtypeStruct(slab, F32),
            jax.ShapeDtypeStruct(slab, F32),
            jax.ShapeDtypeStruct(queries.shape, BF16),
            jax.ShapeDtypeStruct((ROWS, 256), BF16),
        ),
        in_specs=[hbm] * 9 + [vmem] * 2,
        out_specs=(hbm, hbm, hbm, vmem),
        scratch_shapes=[
            pltpu.VMEM(slab, BF16),
            pltpu.VMEM(slab, F32),
            pltpu.VMEM(slab, F32),
            pltpu.VMEM(slab, F32),
            pltpu.VMEM(slab, F32),
            pltpu.VMEM((16, 128), F32),
            pltpu.VMEM((4, 2, ROWS, K_DEV), BF16),
            pltpu.VMEM((8, 2, UNITS, K_DEV), BF16),
            pltpu.VMEM((UNITS, K_DEV), BF16),
            pltpu.VMEM((4, 4, 4, 2, 16, ROWS), BF16),
            pltpu.VMEM((3, 4, 4, 2, 16, ROWS), BF16),
            pltpu.VMEM((4, UNITS, ROWS), BF16),
            pltpu.VMEM((4, UNITS, ROWS), BF16),
            pltpu.VMEM((2, 8, 128), F32),
            pltpu.VMEM((2, 15, 8, 128), F32),
            pltpu.VMEM((8, ROWS), F32),
            pltpu.VMEM((7, 8, ROWS), F32),
            pltpu.VMEM((4, 8, ROWS), F32),
            pltpu.VMEM(queries.shape, BF16),
            pltpu.VMEM((ROWS, 2, 32, 128), BF16),
            pltpu.VMEM(fresh_entries.shape, BF16),
            pltpu.VMEM(queries.shape, BF16),
            pltpu.VMEM((32, 256), F32),
            pltpu.VMEM((4, UNITS, ROWS), F32),
            pltpu.SemaphoreType.DMA((12,)),
            pltpu.SemaphoreType.DMA((N_COPIES,)),
            pltpu.SemaphoreType.DMA((N_COPIES,)),
            pltpu.SemaphoreType.DMA((6,)),
        ],
        compiler_params=pltpu.CompilerParams(
            collective_id=0, has_side_effects=True, vmem_limit_bytes=56 << 20),
        name="step",
    )(gradient, master, first_moment, second_moment, residual,
      norm_gain.reshape(128, 128), queries, layer_cache.reshape(ROWS, 2, 32, 128),
      fresh_entries, lengths.reshape(1, ROWS), shard_table.reshape(1, 32))

    def write(*refs):
        copies = [pltpu.make_async_copy(refs[i], refs[4 + i], refs[8].at[i]) for i in range(4)]
        for copy in copies:
            copy.start()
        for copy in copies:
            copy.wait()

    return pl.pallas_call(
        write,
        out_shape=[jax.ShapeDtypeStruct(r.shape, r.dtype) for r in results],
        in_specs=[hbm] * 4,
        out_specs=[hbm] * 4,
        scratch_shapes=[pltpu.SemaphoreType.DMA((4,))],
        name="write",
    )(*results)


def per_device(gradient, master, first_moment, second_moment, residual, norm_gain,
               queries, layer_cache, fresh_entries, lengths, shard_table):
    entry_count = gradient.size * lax.axis_size("dp") * lax.axis_size("tensor")
    return step(
        gradient, master, first_moment, second_moment, residual, norm_gain,
        queries, layer_cache, fresh_entries, lengths, shard_table,
        CLIP_LEVEL * math.sqrt(entry_count))


def solution(mesh):
    return jax.shard_map(
        per_device,
        mesh=mesh,
        in_specs=(
            P(None, "dp", "tensor"),
            P(None, "dp", "tensor"),
            P(None, "dp", "tensor"),
            P(None, "dp", "tensor"),
            P("dp", "tensor"),
            P(),
            P("dp", "tensor", None),
            P("dp", None, "tensor", None, None),
            P("dp", None, "tensor", None),
            P("dp"),
            P(),
        ),
        out_specs=(
            P(None, "dp", "tensor"),
            P(None, "dp", "tensor"),
            P("dp", "tensor", None),
            P("dp", "tensor"),
        ),
        check_vma=False,
    )
```

```python
import math

import jax
import jax.numpy as jnp
from jax import lax
from jax.experimental import pallas as pl
from jax.experimental.pallas import tpu as pltpu
from jax.sharding import PartitionSpec as P

LEARN_RATE = 0.001
CLIP_LEVEL = 0.5
CLIP_EPSILON = 1e-06
FIRST_DECAY = 0.9
SECOND_DECAY = 0.95
FIRST_CORRECTION = 1.0 - 0.9**10
SECOND_CORRECTION = 1.0 - 0.95**10
ADAM_EPSILON = 1e-08
NORM_EPSILON = 1e-05
SCORE_SCALE = 1.0 / math.sqrt(128)

MESH = pl.DeviceIdType.MESH
F32 = jnp.float32
BF16 = jnp.bfloat16

K_DEV = 2048
ROWS = 256
UNITS = 64
WIDTH = 16384


class Remote:
    def __init__(self, src, dst, sends, recvs, slot, device, arrives=None):
        self.copy = pltpu.make_async_remote_copy(
            src_ref=src, dst_ref=dst, send_sem=sends.at[slot], recv_sem=recvs.at[slot],
            device_id=device, device_id_type=MESH)
        arrives = dst if arrives is None else arrives
        self.inbound = pltpu.make_async_remote_copy(
            src_ref=arrives, dst_ref=arrives, send_sem=sends.at[slot], recv_sem=recvs.at[slot],
            device_id=device, device_id_type=MESH)
        self.copy.start()

    def sent(self):
        self.copy.wait_send()

    def came(self):
        self.inbound.wait_recv()


N_COPIES = 56


def step_kernel(
    clip_limit,
    grad_h, master_h, first_h, second_h, resid_h, gain_h, query_h, cache_h, fresh_h, length_ref, table_ref,
    first_o, second_o, attended_o, act_ref,
    g_v, ma_v, m_v, v_v, gf, gain_v, a_v, b_v, b_swap, c_s, c_r, h_s, h_r,
    p_s, p_r, t_s, t_r, s_g, q_v, kv_v, f_v, len_v, last, pick, load_sem, sends, recvs, many,
):
    d = lax.axis_index("dp")
    t = lax.axis_index("tensor")
    x, zl, y = d // 8, (d // 4) % 2, d % 4
    zh, c = t // 2, t % 2
    oc = 1 - c
    xp, xq = x + 1 - 2 * (x % 2), (x + 3 + 2 * (x % 2)) % 4
    yp, yq = y + 1 - 2 * (y % 2), (y + 3 + 2 * (y % 2)) % 4

    def at(x_, zl_, y_, zh_=None, c_=None):
        zh_ = zh if zh_ is None else zh_
        c_ = c if c_ is None else c_
        return {"dp": x_ * 8 + zl_ * 4 + y_, "tensor": zh_ * 2 + c_}

    to_xp, to_yp, to_diag = at(xp, zl, y), at(x, zl, yp), at(xp, zl, yp)
    to_xq, to_yq, to_zl = at(xq, zl, y), at(x, zl, yq), at(x, 1 - zl, y)
    to_core = at(x, zl, y, zh, oc)

    near = [
        at(x_, z_, y_, zh, c_)
        for x_ in (x, xp) for y_ in (y, yp) for z_ in (zl, 1 - zl) for c_ in (c, oc)
    ][1:]
    far = [
        at(x_, 1 - zl if k == 2 else zl, y_, (zh + k) % 4, c)
        for x_ in (x, xq) for y_ in (y, yq) for k in range(4)
    ][1:]
    team = [at(x, zl, y, (zh + k // 2) % 4, (c + k) % 2) for k in range(1, 8)]

    loads = [
        pltpu.make_async_copy(grad_h, g_v, load_sem.at[0]),
        pltpu.make_async_copy(resid_h, a_v.at[0, c], load_sem.at[1]),
        pltpu.make_async_copy(gain_h.at[pl.ds(pl.multiple_of(t * 16, 16), 16)], gain_v, load_sem.at[2]),
        pltpu.make_async_copy(master_h, ma_v, load_sem.at[3]),
        pltpu.make_async_copy(first_h, m_v, load_sem.at[4]),
        pltpu.make_async_copy(second_h, v_v, load_sem.at[5]),
        pltpu.make_async_copy(query_h, q_v, load_sem.at[6]),
        pltpu.make_async_copy(fresh_h, f_v, load_sem.at[7]),
        pltpu.make_async_copy(cache_h, kv_v, load_sem.at[8]),
    ]
    loads[0].start()
    loads[1].start()
    barrier = pltpu.get_barrier_semaphore()
    greeted = near + far + [team[k] for k in (2, 3, 4, 6)]
    for peer in greeted:
        pl.semaphore_signal(barrier, inc=1, device_id=peer, device_id_type=MESH)

    used = []

    def remote(src, dst, device, arrives=None):
        r = Remote(src, dst, sends, recvs, len(used), device, arrives)
        used.append(r)
        return r

    loads[0].wait()
    for load in loads[2:]:
        load.start()

    def square(i, acc):
        g = g_v[i // 4, pl.ds(pl.multiple_of((i % 4) * 16, 16), 16), :].astype(F32)
        gf[i // 4, pl.ds(pl.multiple_of((i % 4) * 16, 16), 16), :] = g
        sq = g * g
        return acc + (sq[:8] + sq[8:])

    acc = lax.fori_loop(0, 8, square, jnp.zeros((8, K_DEV), F32))
    local = jnp.sum(jnp.sum(acc, axis=0, keepdims=True), axis=1, keepdims=True)
    p_s[0] = jnp.broadcast_to(local, (8, 128))

    pl.semaphore_wait(barrier, len(greeted))

    def to_all(src, dst, peers, pair):
        for k, peer in enumerate(peers):
            pltpu.make_async_remote_copy(
                src_ref=src, dst_ref=dst.at[k], send_sem=many.at[pair], recv_sem=many.at[pair + 1],
                device_id=peer, device_id_type=MESH).start()

    def from_all(dst, pair):
        whole = pltpu.make_async_remote_copy(
            src_ref=dst, dst_ref=dst, send_sem=many.at[pair], recv_sem=many.at[pair + 1],
            device_id=to_core, device_id_type=MESH)
        whole.wait_send()
        whole.wait_recv()

    to_all(p_s.at[0], p_r.at[0], near, 0)

    loads[1].wait()
    def rows_of(slot, half, r):
        return a_v.at[slot, half, pl.ds(r * 128, 128)]

    def to_other_core(slot, r):
        return remote(rows_of(slot, c, r), rows_of(slot, c, r), to_core, rows_of(slot, oc, r))

    rows_x = [remote(rows_of(0, c, r), rows_of(1, c, r), to_xp) for r in range(2)]
    rows_y = [remote(rows_of(0, c, r), rows_of(2, c, r), to_yp) for r in range(2)]
    core_rows = [to_other_core(0, 0), to_other_core(0, 1)]

    own_len = jnp.where(
        lax.broadcasted_iota(jnp.int32, (32, ROWS), 1) // 8
        == lax.broadcasted_iota(jnp.int32, (32, ROWS), 0),
        jnp.broadcast_to(length_ref[...].astype(F32), (32, ROWS)), 0.0).astype(BF16)
    spread_len = jnp.where(
        lax.broadcasted_iota(jnp.int32, (ROWS, 128), 0) % 8
        == lax.broadcasted_iota(jnp.int32, (ROWS, 128), 1) // 16, 1.0, 0.0).astype(BF16)
    len_v[...] = jnp.dot(own_len, spread_len, preferred_element_type=F32)

    def attend_block(g):
        rows = pl.ds(pl.multiple_of(g * 8, 8), 8)
        lane_row = lax.broadcasted_iota(jnp.int32, (32, 128), 1) // 16
        position = lax.broadcasted_iota(jnp.int32, (32, 128), 0).astype(F32)
        own_mine = (lax.broadcasted_iota(jnp.int32, (16, 128), 0)
                    == lax.broadcasted_iota(jnp.int32, (16, 128), 1) // 16)
        q = q_v[rows].reshape(128, 128)
        keys = kv_v[rows, 0].reshape(256, 128)
        values = kv_v[rows, 1].reshape(256, 128)
        own_key = f_v[rows, 0, 0:1].astype(F32).reshape(8, 128)
        own_value = f_v[rows, 0, 1:2].astype(F32).reshape(8, 128)
        own_key = jnp.concatenate([own_key, own_key], axis=0).astype(BF16)
        own_value = jnp.concatenate([own_value, own_value], axis=0).astype(BF16)
        every = lax.dot_general(keys, q, (((1,), (1,)), ((), ())), preferred_element_type=F32)
        own = lax.dot_general(own_key, q, (((1,), (1,)), ((), ())), preferred_element_type=F32)
        scores = every[:32]
        for r in range(1, 8):
            scores = jnp.where(lane_row == r, every[32 * r:32 * r + 32], scores)
        scores = jnp.where(position < len_v[pl.ds(g, 1), :], scores * SCORE_SCALE, -jnp.inf)
        own = jnp.sum(jnp.where(own_mine, own, 0.0), axis=0, keepdims=True) * SCORE_SCALE
        peak = jnp.maximum(jnp.max(scores, axis=0, keepdims=True), own)
        cached = jnp.exp(scores - peak)
        fresh_exp = jnp.exp(own - peak)
        inverse = 1.0 / (jnp.sum(cached, axis=0, keepdims=True) + fresh_exp)
        prob = cached * inverse
        own_prob = jnp.where(own_mine, fresh_exp * inverse, 0.0).astype(BF16)
        wide = jnp.concatenate([jnp.where(lane_row == r, prob, 0.0) for r in range(8)], axis=0).astype(BF16)
        out = lax.dot_general(wide, values, (((0,), (0,)), ((), ())), preferred_element_type=F32)
        out += lax.dot_general(own_prob, own_value, (((0,), (0,)), ((), ())), preferred_element_type=F32)
        attended_o[rows] = out.astype(BF16).reshape(8, 16, 128)

    def attend(first, last):
        @pl.loop(first // 4, last // 4)
        def _(g):
            for i in range(4):
                attend_block(4 * g + i)

    from_all(p_r.at[0], 0)
    total = p_s[0]
    for k in range(15):
        total += p_r[0, k]
    p_s[1] = total
    to_all(p_s.at[1], p_r.at[1], far, 2)

    ones = jnp.ones((8, 512), BF16)
    row_squares = jnp.zeros((8, ROWS), F32)
    for k in range(4):
        r = a_v[0, c, :, k * 512:(k + 1) * 512].astype(F32)
        sq = r * r
        high = sq.astype(BF16)
        low = (sq - high.astype(F32)).astype(BF16)
        for part in (high, low):
            row_squares += lax.dot_general(ones, part, (((1,), (1,)), ((), ())), preferred_element_type=F32)

    t_s[...] = row_squares
    to_all(t_s, t_r, team, 4)

    for load in loads[6:]:
        load.wait()
    attend(0, 8)

    from_all(p_r.at[1], 2)
    total = p_s[1]
    for k in range(15):
        total += p_r[1, k]
    clip = jnp.minimum(1.0, clip_limit / (jnp.sqrt(total) + CLIP_EPSILON))

    for load in loads[2:6]:
        load.wait()
    clip_one = clip[0:1, 0:1]
    gain = jnp.concatenate([gain_v[i:i + 1, :] for i in range(16)], axis=1)

    def fresh(parity, zone):
        row = pl.multiple_of((2 * zone + parity) * 8, 8)
        parts = []
        for i in range(2):
            clipped = gf[i, pl.ds(row, 8), :] * clip_one
            new_first = FIRST_DECAY * m_v[i, pl.ds(row, 8), :] + (1.0 - FIRST_DECAY) * clipped
            new_second = SECOND_DECAY * v_v[i, pl.ds(row, 8), :] + (1.0 - SECOND_DECAY) * clipped * clipped
            step = (new_first * (LEARN_RATE / FIRST_CORRECTION)) / (
                jnp.sqrt(new_second * (1.0 / SECOND_CORRECTION)) + ADAM_EPSILON)
            first_o[i, pl.ds(row, 8), :] = new_first
            second_o[i, pl.ds(row, 8), :] = new_second
            parts.append((ma_v[i, pl.ds(row, 8), :] - step) * gain)
        return jnp.concatenate(parts, axis=0).astype(BF16)

    @pl.loop(0, 4)
    def _(zone):
        b_swap[pl.ds(pl.multiple_of(zone * 16, 16), 16), :] = fresh(oc, zone)

    swap = remote(b_swap, b_v.at[0, c], to_core, b_v.at[0, oc])

    @pl.loop(0, 4)
    def _(zone):
        b_v[0, c, pl.ds(pl.multiple_of(zone * 16, 16), 16), :] = fresh(c, zone)

    def units(src, dst, k, device):
        half = c if k == 0 else oc
        return remote(b_v.at[src, half], b_v.at[dst, half], device)

    unit = {}
    for k in range(2):
        if k == 1:
            swap.came()
        unit[1, k] = units(0, 1, k, to_zl)
        unit[2, k] = units(0, 2, k, to_xq)
        unit[3, k] = units(0, 3, k, to_yq)

    spread = (lax.broadcasted_iota(jnp.int32, (32, 256), 0)
              == lax.broadcasted_iota(jnp.int32, (32, 256), 1) // 8).astype(F32).astype(BF16)
    table = jnp.broadcast_to(table_ref[...].astype(F32), (8, 32)).astype(BF16)
    wanted = jnp.dot(table, spread, preferred_element_type=F32)
    same_unit = (lax.broadcasted_iota(jnp.int32, (8, 256), 0)
                 == lax.broadcasted_iota(jnp.int32, (8, 256), 1) % 8)
    for group in range(4):
        gx, gy = (xp if group % 2 else x), (yp if group // 2 else y)
        for pair in range(4):
            halves = []
            for block in (2 * pair, 2 * pair + 1):
                bx = (gx + 3 + 2 * (gx % 2)) % 4 if block in (2, 4, 6, 7) else gx
                by = (gy + 3 + 2 * (gy % 2)) % 4 if block in (3, 5, 6, 7) else gy
                bz = 1 - zl if block in (1, 4, 5, 7) else zl
                shard = (bx * 8 + bz * 4 + by).astype(F32)
                halves.append(jnp.where(same_unit & (wanted == shard), 1.0, 0.0))
            row = group * 64 + pair * 16
            pick[row:row + 16, :] = jnp.concatenate(halves, axis=0).astype(BF16)

    from_all(t_r, 4)
    squares = t_s[...]
    for k in range(7):
        squares += t_r[k]
    s_g[0] = squares
    square_copies = [remote(s_g.at[0], s_g.at[slot], device) for slot, device in ((1, to_xp), (2, to_yp), (3, to_diag))]
    attend(8, 32)

    core_got = []
    diag = []

    def pass_rows(r):
        rows_x[r].came()
        core_got.append(to_other_core(1, r))
        if r == 0:
            diag.append(remote(rows_of(1, c, 0), rows_of(3, c, 0), to_yp))
        rows_y[r].came()
        core_got.append(to_other_core(2, r))
        if r == 1:
            diag.append(remote(rows_of(2, c, 1), rows_of(3, c, 1), to_xp))

    pass_rows(0)
    for k in range(2):
        unit[1, k].came()
        unit[4, k] = units(1, 4, k, to_xq)
        unit[5, k] = units(1, 5, k, to_yq)
    unit[2, 0].came()
    unit[6, 0] = units(2, 6, 0, to_yq)
    unit[3, 0].came()
    unit[3, 1].came()
    unit[6, 1] = units(3, 6, 1, to_xq)
    unit[2, 1].came()
    pass_rows(1)
    for r in core_rows + core_got:
        r.came()

    def half_product(slot, count, a, h):
        lhs = b_v[slot:slot + count, h].reshape(count * UNITS, K_DEV)
        return lax.dot_general(lhs, a_v[a, h], (((1,), (1,)), ((), ())), preferred_element_type=F32)

    def product(slot, count, a):
        out = half_product(slot, count, a, 0) + half_product(slot, count, a, 1)
        return out.reshape(count, 4, 16, ROWS).astype(BF16)

    def tile(p, pairs, a):
        out = product(2 * p, 2 * pairs, a)
        for i in range(pairs):
            for z in range(4):
                c_s[p + i, z, a] = out[2 * i:2 * i + 2, z]

    sums = []

    def send_sums(view_s, view_r):
        for k in range(1, 4):
            z = (zh + k) % 4
            sums.append(remote(view_s(z), view_r(k - 1), at(x, zl, y, z, c)))

    @pl.loop(0, 3)
    def _(a):
        tile(0, 2, a)

    send_sums(lambda z: c_s.at[pl.ds(0, 2), z, pl.ds(0, 3)], lambda k: c_r.at[k, pl.ds(0, 2), pl.ds(0, 3)])
    unit[4, 0].came()
    unit[7, 0] = units(4, 7, 0, to_yq)
    unit[5, 0].came()
    unit[5, 1].came()
    unit[7, 1] = units(5, 7, 1, to_xq)
    unit[4, 1].came()

    @pl.loop(0, 3)
    def _(a):
        tile(2, 1, a)

    send_sums(lambda z: c_s.at[2, z, pl.ds(0, 3)], lambda k: c_r.at[k, 2, pl.ds(0, 3)])
    last_rows = []
    for r in range(2):
        diag[r].came()
        last_rows.append(to_other_core(3, r))
    for r in last_rows:
        r.came()
    tile(0, 2, 3)
    tile(2, 1, 3)
    send_sums(lambda z: c_s.at[pl.ds(0, 3), z, 3], lambda k: c_r.at[k, pl.ds(0, 3), 3])

    for k in range(2):
        unit[6, k].came()

    @pl.loop(0, 4)
    def _(a):
        out = product(6, 1, a)
        for z in range(4):
            c_s[3, z, a, 0] = out[0, z]

    send_sums(lambda z: c_s.at[3, z, :, 0], lambda k: c_r.at[k, 3, :, 0])

    unit[7, 0].came()

    @pl.loop(0, 4)
    def _(a):
        last[a] = half_product(7, 1, a, c)

    unit[7, 1].came()

    @pl.loop(0, 4)
    def _(a):
        out = (last[a] + half_product(7, 1, a, oc)).reshape(4, 16, ROWS).astype(BF16)
        for z in range(4):
            c_s[3, z, a, 1] = out[z]

    send_sums(lambda z: c_s.at[3, z, :, 1], lambda k: c_r.at[k, 3, :, 1])

    for r in square_copies:
        r.came()

    def activations(a, p):
        scale = lax.rsqrt(s_g[a][0:1, :] * (1.0 / WIDTH) + NORM_EPSILON)
        v = c_s[p, zh, a].astype(F32)
        for k in range(3):
            v += c_r[k, p, a].astype(F32)
        gate = v[:, :8] * scale
        up = v[:, 8:] * scale
        hidden = (gate / (1.0 + jnp.exp(-gate)) * up).reshape(16, ROWS).astype(BF16)
        h_s[a, p * 16:(p + 1) * 16, :] = hidden

    for r in sums[:9]:
        r.came()
    for a in range(4):
        for p in range(3):
            activations(a, p)
    for r in sums[9:]:
        r.came()
    outs = []
    for a, device in ((3, to_diag), (1, to_xp), (2, to_yp)):
        activations(a, 3)
        outs.append(remote(h_s.at[a], h_r.at[a], device))
    activations(0, 3)
    h_r[0] = h_s[0]
    for r in outs:
        r.came()
    act_ref[...] = lax.dot_general(
        h_r[...].reshape(256, ROWS), pick[...], (((0,), (0,)), ((), ())), preferred_element_type=F32).astype(BF16)

    for r in used:
        r.sent()
    assert len(used) <= N_COPIES, len(used)


def step(gradient, master, first_moment, second_moment, residual, norm_gain,
         queries, layer_cache, fresh_entries, lengths, shard_table, clip_limit):
    hbm = pl.BlockSpec(memory_space=pl.ANY)
    vmem = pl.BlockSpec(memory_space=pltpu.VMEM)
    slab = gradient.shape

    def kernel(*refs):
        step_kernel(clip_limit, *refs)

    results = pl.pallas_call(
        kernel,
        out_shape=(
            pltpu.VMEM(slab, F32),
            pltpu.VMEM(slab, F32),
            pltpu.VMEM(queries.shape, BF16),
            pltpu.VMEM((ROWS, 256), BF16),
        ),
        in_specs=[hbm] * 9 + [vmem] * 2,
        out_specs=(vmem,) * 4,
        scratch_shapes=[
            pltpu.VMEM(slab, BF16),
            pltpu.VMEM(slab, F32),
            pltpu.VMEM(slab, F32),
            pltpu.VMEM(slab, F32),
            pltpu.VMEM(slab, F32),
            pltpu.VMEM((16, 128), F32),
            pltpu.VMEM((4, 2, ROWS, K_DEV), BF16),
            pltpu.VMEM((8, 2, UNITS, K_DEV), BF16),
            pltpu.VMEM((UNITS, K_DEV), BF16),
            pltpu.VMEM((4, 4, 4, 2, 16, ROWS), BF16),
            pltpu.VMEM((3, 4, 4, 2, 16, ROWS), BF16),
            pltpu.VMEM((4, UNITS, ROWS), BF16),
            pltpu.VMEM((4, UNITS, ROWS), BF16),
            pltpu.VMEM((2, 8, 128), F32),
            pltpu.VMEM((2, 15, 8, 128), F32),
            pltpu.VMEM((8, ROWS), F32),
            pltpu.VMEM((7, 8, ROWS), F32),
            pltpu.VMEM((4, 8, ROWS), F32),
            pltpu.VMEM(queries.shape, BF16),
            pltpu.VMEM((ROWS, 2, 32, 128), BF16),
            pltpu.VMEM((ROWS, 1, 2, 128), BF16),
            pltpu.VMEM((32, 128), F32),
            pltpu.VMEM((4, UNITS, ROWS), F32),
            pltpu.VMEM((256, 256), BF16),
            pltpu.SemaphoreType.DMA((9,)),
            pltpu.SemaphoreType.DMA((N_COPIES,)),
            pltpu.SemaphoreType.DMA((N_COPIES,)),
            pltpu.SemaphoreType.DMA((6,)),
        ],
        compiler_params=pltpu.CompilerParams(
            collective_id=0, has_side_effects=True, vmem_limit_bytes=56 << 20),
        name="step",
    )(gradient, master, first_moment, second_moment, residual,
      norm_gain.reshape(128, 128), queries, layer_cache.reshape(ROWS, 2, 32, 128),
      fresh_entries.transpose(0, 2, 1, 3), lengths.reshape(1, ROWS), shard_table.reshape(1, 32))

    def write(*refs):
        copies = [pltpu.make_async_copy(refs[i], refs[4 + i], refs[8].at[i]) for i in range(4)]
        for copy in copies:
            copy.start()
        for copy in copies:
            copy.wait()

    return pl.pallas_call(
        write,
        out_shape=[jax.ShapeDtypeStruct(r.shape, r.dtype) for r in results],
        in_specs=[vmem] * 4,
        out_specs=[hbm] * 4,
        scratch_shapes=[pltpu.SemaphoreType.DMA((4,))],
        name="write",
    )(*[pltpu.with_memory_space_constraint(r, pltpu.VMEM) for r in results])


def per_device(gradient, master, first_moment, second_moment, residual, norm_gain,
               queries, layer_cache, fresh_entries, lengths, shard_table):
    entry_count = gradient.size * lax.axis_size("dp") * lax.axis_size("tensor")
    return step(
        gradient, master, first_moment, second_moment, residual, norm_gain,
        queries, layer_cache, fresh_entries, lengths, shard_table,
        CLIP_LEVEL * math.sqrt(entry_count))


def solution(mesh):
    return jax.shard_map(
        per_device,
        mesh=mesh,
        in_specs=(
            P(None, "dp", "tensor"),
            P(None, "dp", "tensor"),
            P(None, "dp", "tensor"),
            P(None, "dp", "tensor"),
            P("dp", "tensor"),
            P(),
            P("dp", "tensor", None),
            P("dp", None, "tensor", None, None),
            P("dp", None, "tensor", None),
            P("dp"),
            P(),
        ),
        out_specs=(
            P(None, "dp", "tensor"),
            P(None, "dp", "tensor"),
            P("dp", "tensor", None),
            P("dp", "tensor"),
        ),
        check_vma=False,
    )
```

```python
import math

import jax
import jax.numpy as jnp
from jax import lax
from jax.experimental import pallas as pl
from jax.experimental.pallas import tpu as pltpu
from jax.sharding import PartitionSpec as P

LEARN_RATE = 0.001
CLIP_LEVEL = 0.5
CLIP_EPSILON = 1e-06
FIRST_DECAY = 0.9
SECOND_DECAY = 0.95
FIRST_CORRECTION = 1.0 - 0.9**10
SECOND_CORRECTION = 1.0 - 0.95**10
ADAM_EPSILON = 1e-08
NORM_EPSILON = 1e-05
SCORE_SCALE = 1.0 / math.sqrt(128)

MESH = pl.DeviceIdType.MESH
F32 = jnp.float32
BF16 = jnp.bfloat16

K_DEV = 2048
ROWS = 256
UNITS = 64
WIDTH = 16384


class Remote:
    def __init__(self, src, dst, sends, recvs, slot, device, arrives=None):
        self.copy = pltpu.make_async_remote_copy(
            src_ref=src, dst_ref=dst, send_sem=sends.at[slot], recv_sem=recvs.at[slot],
            device_id=device, device_id_type=MESH)
        arrives = dst if arrives is None else arrives
        self.inbound = pltpu.make_async_remote_copy(
            src_ref=arrives, dst_ref=arrives, send_sem=sends.at[slot], recv_sem=recvs.at[slot],
            device_id=device, device_id_type=MESH)
        self.copy.start()

    def sent(self):
        self.copy.wait_send()

    def came(self):
        self.inbound.wait_recv()


N_COPIES = 56


def step_kernel(
    clip_limit,
    grad_h, master_h, first_h, second_h, resid_h, gain_h, query_h, cache_h, fresh_h, length_h, table_h,
    first_o, second_o, attended_o, act_ref,
    g_v, ma_v, m_v, v_v, gf, gain_v, a_v, b_v, b_swap, c_s, c_r, h_s, h_r,
    p_s, p_r, t_s, t_r, s_g, q_v, kv_v, f_v, len_v, last, pick, length_ref, table_ref, load_sem, quarter_sem, sends, recvs, many,
):
    d = lax.axis_index("dp")
    t = lax.axis_index("tensor")
    x, zl, y = d // 8, (d // 4) % 2, d % 4
    zh, c = t // 2, t % 2
    oc = 1 - c
    xp, xq = x + 1 - 2 * (x % 2), (x + 3 + 2 * (x % 2)) % 4
    yp, yq = y + 1 - 2 * (y % 2), (y + 3 + 2 * (y % 2)) % 4

    def at(x_, zl_, y_, zh_=None, c_=None):
        zh_ = zh if zh_ is None else zh_
        c_ = c if c_ is None else c_
        return {"dp": x_ * 8 + zl_ * 4 + y_, "tensor": zh_ * 2 + c_}

    to_xp, to_yp, to_diag = at(xp, zl, y), at(x, zl, yp), at(xp, zl, yp)
    to_xq, to_yq, to_zl = at(xq, zl, y), at(x, zl, yq), at(x, 1 - zl, y)
    to_core = at(x, zl, y, zh, oc)

    near = [
        at(x_, z_, y_, zh, c_)
        for x_ in (x, xp) for y_ in (y, yp) for z_ in (zl, 1 - zl) for c_ in (c, oc)
    ][1:]
    far = [
        at(x_, 1 - zl if k == 2 else zl, y_, (zh + k) % 4, c)
        for x_ in (x, xq) for y_ in (y, yq) for k in range(4)
    ][1:]
    team = [at(x, zl, y, (zh + k // 2) % 4, (c + k) % 2) for k in range(1, 8)]

    loads = [
        None,
        pltpu.make_async_copy(resid_h, a_v.at[0, c], load_sem.at[1]),
        pltpu.make_async_copy(gain_h.at[pl.ds(pl.multiple_of(t * 16, 16), 16)], gain_v, load_sem.at[2]),
        pltpu.make_async_copy(master_h, ma_v, load_sem.at[3]),
        pltpu.make_async_copy(first_h, m_v, load_sem.at[4]),
        pltpu.make_async_copy(second_h, v_v, load_sem.at[5]),
        pltpu.make_async_copy(query_h, q_v, load_sem.at[6]),
        pltpu.make_async_copy(fresh_h, f_v, load_sem.at[7]),
        pltpu.make_async_copy(cache_h, kv_v, load_sem.at[8]),
        pltpu.make_async_copy(length_h, length_ref, load_sem.at[9]),
        pltpu.make_async_copy(table_h, table_ref, load_sem.at[10]),
    ]
    quarters = [
        pltpu.make_async_copy(
            grad_h.at[k // 2, pl.ds(k % 2 * 32, 32)], g_v.at[k // 2, pl.ds(k % 2 * 32, 32)], quarter_sem.at[k])
        for k in range(4)
    ]
    for quarter in quarters:
        quarter.start()
    loads[1].start()
    barrier = pltpu.get_barrier_semaphore()
    greeted = near + far + [team[k] for k in (2, 3, 4, 6)]
    for peer in greeted:
        pl.semaphore_signal(barrier, inc=1, device_id=peer, device_id_type=MESH)

    used = []

    def remote(src, dst, device, arrives=None):
        r = Remote(src, dst, sends, recvs, len(used), device, arrives)
        used.append(r)
        return r

    acc = jnp.zeros((8, K_DEV), F32)
    for k in range(4):
        quarters[k].wait()
        if k == 0:
            for load in loads[2:]:
                load.start()
        for r in range(2):
            rows = pl.ds(k % 2 * 32 + r * 16, 16)
            g = g_v[k // 2, rows, :].astype(F32)
            gf[k // 2, rows, :] = g
            sq = g * g
            acc += sq[:8] + sq[8:]
    local = jnp.sum(jnp.sum(acc, axis=0, keepdims=True), axis=1, keepdims=True)
    p_s[0] = jnp.broadcast_to(local, (1, 128))

    pl.semaphore_wait(barrier, len(greeted))

    def to_all(src, dst, peers, pair):
        for k, peer in enumerate(peers):
            pltpu.make_async_remote_copy(
                src_ref=src, dst_ref=dst.at[k], send_sem=many.at[pair], recv_sem=many.at[pair + 1],
                device_id=peer, device_id_type=MESH).start()

    def from_all(dst, pair):
        whole = pltpu.make_async_remote_copy(
            src_ref=dst, dst_ref=dst, send_sem=many.at[pair], recv_sem=many.at[pair + 1],
            device_id=to_core, device_id_type=MESH)
        whole.wait_send()
        whole.wait_recv()

    to_all(p_s.at[0], p_r.at[0], near, 0)

    loads[1].wait()
    def rows_of(slot, half, r):
        return a_v.at[slot, half, pl.ds(r * 128, 128)]

    def to_other_core(slot, r):
        return remote(rows_of(slot, c, r), rows_of(slot, c, r), to_core, rows_of(slot, oc, r))

    rows_x = [remote(rows_of(0, c, r), rows_of(1, c, r), to_xp) for r in range(2)]
    rows_y = [remote(rows_of(0, c, r), rows_of(2, c, r), to_yp) for r in range(2)]
    core_rows = [to_other_core(0, 0), to_other_core(0, 1)]

    def attend_block(g):
        rows = pl.ds(pl.multiple_of(g * 8, 8), 8)
        lane_row = lax.broadcasted_iota(jnp.int32, (32, 128), 1) // 16
        position = lax.broadcasted_iota(jnp.int32, (32, 128), 0).astype(F32)
        own_mine = (lax.broadcasted_iota(jnp.int32, (16, 128), 0)
                    == lax.broadcasted_iota(jnp.int32, (16, 128), 1) // 16)
        q = q_v[rows].reshape(128, 128)
        keys = kv_v[rows, 0].reshape(256, 128)
        values = kv_v[rows, 1].reshape(256, 128)
        own_key = f_v[rows, 0, 0:1].astype(F32).reshape(8, 128)
        own_value = f_v[rows, 0, 1:2].astype(F32).reshape(8, 128)
        own_key = jnp.concatenate([own_key, own_key], axis=0).astype(BF16)
        own_value = jnp.concatenate([own_value, own_value], axis=0).astype(BF16)
        every = lax.dot_general(keys, q, (((1,), (1,)), ((), ())), preferred_element_type=F32)
        own = lax.dot_general(own_key, q, (((1,), (1,)), ((), ())), preferred_element_type=F32)
        scores = every[:32]
        for r in range(1, 8):
            scores = jnp.where(lane_row == r, every[32 * r:32 * r + 32], scores)
        scores = jnp.where(position < len_v[pl.ds(g, 1), :], scores * SCORE_SCALE, -jnp.inf)
        own = jnp.sum(jnp.where(own_mine, own, 0.0), axis=0, keepdims=True) * SCORE_SCALE
        peak = jnp.maximum(jnp.max(scores, axis=0, keepdims=True), own)
        cached = jnp.exp(scores - peak)
        fresh_exp = jnp.exp(own - peak)
        inverse = 1.0 / (jnp.sum(cached, axis=0, keepdims=True) + fresh_exp)
        prob = cached * inverse
        own_prob = jnp.where(own_mine, fresh_exp * inverse, 0.0).astype(BF16)
        wide = jnp.concatenate([jnp.where(lane_row == r, prob, 0.0) for r in range(8)], axis=0).astype(BF16)
        out = lax.dot_general(wide, values, (((0,), (0,)), ((), ())), preferred_element_type=F32)
        out += lax.dot_general(own_prob, own_value, (((0,), (0,)), ((), ())), preferred_element_type=F32)
        attended_o[rows] = out.astype(BF16).reshape(8, 16, 128)

    def attend(first, last):
        @pl.loop(first // 4, last // 4)
        def _(g):
            for i in range(4):
                attend_block(4 * g + i)

    from_all(p_r.at[0], 0)
    total = p_s[0]
    for k in range(15):
        total += p_r[0, k]
    p_s[1] = total
    to_all(p_s.at[1], p_r.at[1], far, 2)

    ones = jnp.ones((8, 512), BF16)
    row_squares = jnp.zeros((8, ROWS), F32)
    for k in range(4):
        r = a_v[0, c, :, k * 512:(k + 1) * 512].astype(F32)
        sq = r * r
        high = sq.astype(BF16)
        low = (sq - high.astype(F32)).astype(BF16)
        for part in (high, low):
            row_squares += lax.dot_general(ones, part, (((1,), (1,)), ((), ())), preferred_element_type=F32)

    t_s[...] = row_squares[0:1, :]
    to_all(t_s, t_r, team, 4)

    for load in loads[6:]:
        load.wait()
    own_len = jnp.where(
        lax.broadcasted_iota(jnp.int32, (32, ROWS), 1) // 8
        == lax.broadcasted_iota(jnp.int32, (32, ROWS), 0),
        jnp.broadcast_to(length_ref[...].astype(F32), (32, ROWS)), 0.0).astype(BF16)
    spread_len = jnp.where(
        lax.broadcasted_iota(jnp.int32, (ROWS, 128), 0) % 8
        == lax.broadcasted_iota(jnp.int32, (ROWS, 128), 1) // 16, 1.0, 0.0).astype(BF16)
    len_v[...] = jnp.dot(own_len, spread_len, preferred_element_type=F32)
    attend(0, 8)

    from_all(p_r.at[1], 2)
    total = p_s[1]
    for k in range(15):
        total += p_r[1, k]
    clip = jnp.minimum(1.0, clip_limit / (jnp.sqrt(total) + CLIP_EPSILON))

    for load in loads[2:6]:
        load.wait()
    clip_one = clip[0:1, 0:1]
    gain = jnp.concatenate([gain_v[i:i + 1, :] for i in range(16)], axis=1)

    def fresh(parity, zone):
        row = pl.multiple_of((2 * zone + parity) * 8, 8)
        parts = []
        for i in range(2):
            clipped = gf[i, pl.ds(row, 8), :] * clip_one
            new_first = FIRST_DECAY * m_v[i, pl.ds(row, 8), :] + (1.0 - FIRST_DECAY) * clipped
            new_second = SECOND_DECAY * v_v[i, pl.ds(row, 8), :] + (1.0 - SECOND_DECAY) * clipped * clipped
            step = (new_first * (LEARN_RATE / FIRST_CORRECTION)) / (
                jnp.sqrt(new_second * (1.0 / SECOND_CORRECTION)) + ADAM_EPSILON)
            first_o[i, pl.ds(row, 8), :] = new_first
            second_o[i, pl.ds(row, 8), :] = new_second
            parts.append((ma_v[i, pl.ds(row, 8), :] - step) * gain)
        return jnp.concatenate(parts, axis=0).astype(BF16)

    @pl.loop(0, 4)
    def _(zone):
        b_v[0, c, pl.ds(pl.multiple_of(zone * 16, 16), 16), :] = fresh(c, zone)

    def units(src, dst, k, device):
        half = c if k == 0 else oc
        return remote(b_v.at[src, half], b_v.at[dst, half], device)

    unit = {}

    def units_out(k):
        unit[1, k] = units(0, 1, k, to_zl)
        unit[2, k] = units(0, 2, k, to_xq)
        unit[3, k] = units(0, 3, k, to_yq)

    units_out(0)

    @pl.loop(0, 4)
    def _(zone):
        b_swap[pl.ds(pl.multiple_of(zone * 16, 16), 16), :] = fresh(oc, zone)

    swap = remote(b_swap, b_v.at[0, c], to_core, b_v.at[0, oc])
    swap.came()
    units_out(1)

    spread = (lax.broadcasted_iota(jnp.int32, (32, 256), 0)
              == lax.broadcasted_iota(jnp.int32, (32, 256), 1) // 8).astype(F32).astype(BF16)
    table = jnp.broadcast_to(table_ref[...].astype(F32), (8, 32)).astype(BF16)
    wanted = jnp.dot(table, spread, preferred_element_type=F32)
    same_unit = (lax.broadcasted_iota(jnp.int32, (8, 256), 0)
                 == lax.broadcasted_iota(jnp.int32, (8, 256), 1) % 8)
    for group in range(4):
        gx, gy = (xp if group % 2 else x), (yp if group // 2 else y)
        for pair in range(4):
            halves = []
            for block in (2 * pair, 2 * pair + 1):
                bx = (gx + 3 + 2 * (gx % 2)) % 4 if block in (2, 4, 6, 7) else gx
                by = (gy + 3 + 2 * (gy % 2)) % 4 if block in (3, 5, 6, 7) else gy
                bz = 1 - zl if block in (1, 4, 5, 7) else zl
                shard = (bx * 8 + bz * 4 + by).astype(F32)
                halves.append(jnp.where(same_unit & (wanted == shard), 1.0, 0.0))
            row = group * 64 + pair * 16
            pick[row:row + 16, :] = jnp.concatenate(halves, axis=0).astype(BF16)

    from_all(t_r, 4)
    squares = t_s[...]
    for k in range(7):
        squares += t_r[k]
    s_g[0] = squares
    square_copies = [remote(s_g.at[0], s_g.at[slot], device) for slot, device in ((1, to_xp), (2, to_yp), (3, to_diag))]
    attend(8, 32)

    core_got = []
    diag = []

    def pass_rows(r):
        rows_x[r].came()
        core_got.append(to_other_core(1, r))
        if r == 0:
            diag.append(remote(rows_of(1, c, 0), rows_of(3, c, 0), to_yp))
        rows_y[r].came()
        core_got.append(to_other_core(2, r))
        if r == 1:
            diag.append(remote(rows_of(2, c, 1), rows_of(3, c, 1), to_xp))

    pass_rows(0)
    for k in range(2):
        unit[1, k].came()
        unit[4, k] = units(1, 4, k, to_xq)
        unit[5, k] = units(1, 5, k, to_yq)
    unit[2, 0].came()
    unit[6, 0] = units(2, 6, 0, to_yq)
    unit[3, 0].came()
    unit[3, 1].came()
    unit[6, 1] = units(3, 6, 1, to_xq)
    unit[2, 1].came()
    def half_product(slot, count, a, h):
        lhs = b_v[slot:slot + count, h].reshape(count * UNITS, K_DEV)
        return lax.dot_general(lhs, a_v[a, h], (((1,), (1,)), ((), ())), preferred_element_type=F32)

    def product(slot, count, a):
        out = half_product(slot, count, a, 0) + half_product(slot, count, a, 1)
        return out.reshape(count, 4, 16, ROWS).astype(BF16)

    def tile(p, pairs, a):
        out = product(2 * p, 2 * pairs, a)
        for i in range(pairs):
            for z in range(4):
                c_s[p + i, z, a] = out[2 * i:2 * i + 2, z]

    sums = []

    def send_sums(view_s, view_r):
        for k in range(1, 4):
            z = (zh + k) % 4
            sums.append(remote(view_s(z), view_r(k - 1), at(x, zl, y, z, c)))

    for r in core_rows:
        r.came()
    tile(0, 2, 0)
    send_sums(lambda z: c_s.at[pl.ds(0, 2), z, 0], lambda k: c_r.at[k, pl.ds(0, 2), 0])
    pass_rows(1)
    for r in core_got:
        r.came()

    @pl.loop(1, 3)
    def _(a):
        tile(0, 2, a)

    send_sums(lambda z: c_s.at[pl.ds(0, 2), z, pl.ds(1, 2)], lambda k: c_r.at[k, pl.ds(0, 2), pl.ds(1, 2)])
    unit[4, 0].came()
    unit[7, 0] = units(4, 7, 0, to_yq)
    unit[5, 0].came()
    unit[5, 1].came()
    unit[7, 1] = units(5, 7, 1, to_xq)
    unit[4, 1].came()

    @pl.loop(0, 3)
    def _(a):
        tile(2, 1, a)

    send_sums(lambda z: c_s.at[2, z, pl.ds(0, 3)], lambda k: c_r.at[k, 2, pl.ds(0, 3)])
    last_rows = []
    for r in range(2):
        diag[r].came()
        last_rows.append(to_other_core(3, r))
    for r in last_rows:
        r.came()
    tile(0, 2, 3)
    tile(2, 1, 3)
    send_sums(lambda z: c_s.at[pl.ds(0, 3), z, 3], lambda k: c_r.at[k, pl.ds(0, 3), 3])

    for k in range(2):
        unit[6, k].came()

    @pl.loop(0, 4)
    def _(a):
        out = product(6, 1, a)
        for z in range(4):
            c_s[3, z, a, 0] = out[0, z]

    send_sums(lambda z: c_s.at[3, z, :, 0], lambda k: c_r.at[k, 3, :, 0])

    unit[7, 0].came()

    @pl.loop(0, 4)
    def _(a):
        last[a] = half_product(7, 1, a, c)

    unit[7, 1].came()

    @pl.loop(0, 4)
    def _(a):
        out = (last[a] + half_product(7, 1, a, oc)).reshape(4, 16, ROWS).astype(BF16)
        for z in range(4):
            c_s[3, z, a, 1] = out[z]

    send_sums(lambda z: c_s.at[3, z, :, 1], lambda k: c_r.at[k, 3, :, 1])

    for r in square_copies:
        r.came()

    def activations(a, p):
        scale = lax.rsqrt(s_g[a] * (1.0 / WIDTH) + NORM_EPSILON)
        v = c_s[p, zh, a].astype(F32)
        for k in range(3):
            v += c_r[k, p, a].astype(F32)
        gate = v[:, :8] * scale
        up = v[:, 8:] * scale
        hidden = (gate / (1.0 + jnp.exp(-gate)) * up).reshape(16, ROWS).astype(BF16)
        h_s[a, p * 16:(p + 1) * 16, :] = hidden

    for r in sums[:12]:
        r.came()
    outs = []
    for a, device in ((3, to_diag), (1, to_xp), (2, to_yp), (0, None)):
        for p in range(3):
            activations(a, p)
        if device is not None:
            outs.append(remote(h_s.at[a, pl.ds(0, 48)], h_r.at[a, pl.ds(0, 48)], device))
    for r in sums[12:]:
        r.came()
    for a, device in ((3, to_diag), (1, to_xp), (2, to_yp)):
        activations(a, 3)
        outs.append(remote(h_s.at[a, pl.ds(48, 16)], h_r.at[a, pl.ds(48, 16)], device))
    activations(0, 3)
    h_r[0] = h_s[0]
    for r in outs:
        r.came()
    act_ref[...] = lax.dot_general(
        h_r[...].reshape(256, ROWS), pick[...], (((0,), (0,)), ((), ())), preferred_element_type=F32).astype(BF16)

    for r in used:
        r.sent()
    assert len(used) <= N_COPIES, len(used)


def step(gradient, master, first_moment, second_moment, residual, norm_gain,
         queries, layer_cache, fresh_entries, lengths, shard_table, clip_limit):
    hbm = pl.BlockSpec(memory_space=pl.ANY)
    vmem = pl.BlockSpec(memory_space=pltpu.VMEM)
    slab = gradient.shape

    def kernel(*refs):
        step_kernel(clip_limit, *refs)

    results = pl.pallas_call(
        kernel,
        out_shape=(
            pltpu.VMEM(slab, F32),
            pltpu.VMEM(slab, F32),
            pltpu.VMEM(queries.shape, BF16),
            pltpu.VMEM((ROWS, 256), BF16),
        ),
        in_specs=[hbm] * 11,
        out_specs=(vmem,) * 4,
        scratch_shapes=[
            pltpu.VMEM(slab, BF16),
            pltpu.VMEM(slab, F32),
            pltpu.VMEM(slab, F32),
            pltpu.VMEM(slab, F32),
            pltpu.VMEM(slab, F32),
            pltpu.VMEM((16, 128), F32),
            pltpu.VMEM((4, 2, ROWS, K_DEV), BF16),
            pltpu.VMEM((8, 2, UNITS, K_DEV), BF16),
            pltpu.VMEM((UNITS, K_DEV), BF16),
            pltpu.VMEM((4, 4, 4, 2, 16, ROWS), BF16),
            pltpu.VMEM((3, 4, 4, 2, 16, ROWS), BF16),
            pltpu.VMEM((4, UNITS, ROWS), BF16),
            pltpu.VMEM((4, UNITS, ROWS), BF16),
            pltpu.VMEM((2, 1, 128), F32),
            pltpu.VMEM((2, 15, 1, 128), F32),
            pltpu.VMEM((1, ROWS), F32),
            pltpu.VMEM((7, 1, ROWS), F32),
            pltpu.VMEM((4, 1, ROWS), F32),
            pltpu.VMEM(queries.shape, BF16),
            pltpu.VMEM((ROWS, 2, 32, 128), BF16),
            pltpu.VMEM((ROWS, 1, 2, 128), BF16),
            pltpu.VMEM((32, 128), F32),
            pltpu.VMEM((4, UNITS, ROWS), F32),
            pltpu.VMEM((256, 256), BF16),
            pltpu.VMEM((1, ROWS), jnp.int32),
            pltpu.VMEM((1, 32), jnp.int32),
            pltpu.SemaphoreType.DMA((11,)),
            pltpu.SemaphoreType.DMA((4,)),
            pltpu.SemaphoreType.DMA((N_COPIES,)),
            pltpu.SemaphoreType.DMA((N_COPIES,)),
            pltpu.SemaphoreType.DMA((6,)),
        ],
        compiler_params=pltpu.CompilerParams(
            collective_id=0, has_side_effects=True, vmem_limit_bytes=56 << 20),
        name="step",
    )(gradient, master, first_moment, second_moment, residual,
      norm_gain.reshape(128, 128), queries, layer_cache.reshape(ROWS, 2, 32, 128),
      fresh_entries.transpose(0, 2, 1, 3), lengths.reshape(1, ROWS), shard_table.reshape(1, 32))

    def write(*refs):
        copies = [pltpu.make_async_copy(refs[i], refs[4 + i], refs[8].at[i]) for i in range(4)]
        for copy in copies:
            copy.start()
        for copy in copies:
            copy.wait()

    return pl.pallas_call(
        write,
        out_shape=[jax.ShapeDtypeStruct(r.shape, r.dtype) for r in results],
        in_specs=[vmem] * 4,
        out_specs=[hbm] * 4,
        scratch_shapes=[pltpu.SemaphoreType.DMA((4,))],
        name="write",
    )(*[pltpu.with_memory_space_constraint(r, pltpu.VMEM) for r in results])


def per_device(gradient, master, first_moment, second_moment, residual, norm_gain,
               queries, layer_cache, fresh_entries, lengths, shard_table):
    entry_count = gradient.size * lax.axis_size("dp") * lax.axis_size("tensor")
    return step(
        gradient, master, first_moment, second_moment, residual, norm_gain,
        queries, layer_cache, fresh_entries, lengths, shard_table,
        CLIP_LEVEL * math.sqrt(entry_count))


def solution(mesh):
    return jax.shard_map(
        per_device,
        mesh=mesh,
        in_specs=(
            P(None, "dp", "tensor"),
            P(None, "dp", "tensor"),
            P(None, "dp", "tensor"),
            P(None, "dp", "tensor"),
            P("dp", "tensor"),
            P(),
            P("dp", "tensor", None),
            P("dp", None, "tensor", None, None),
            P("dp", None, "tensor", None),
            P("dp"),
            P(),
        ),
        out_specs=(
            P(None, "dp", "tensor"),
            P(None, "dp", "tensor"),
            P("dp", "tensor", None),
            P("dp", "tensor"),
        ),
        check_vma=False,
    )
```

```python
import math

import jax
import jax.numpy as jnp
from jax import lax
from jax.experimental import pallas as pl
from jax.experimental.pallas import tpu as pltpu
from jax.sharding import PartitionSpec as P

LEARN_RATE = 0.001
CLIP_LEVEL = 0.5
CLIP_EPSILON = 1e-06
FIRST_DECAY = 0.9
SECOND_DECAY = 0.95
FIRST_CORRECTION = 1.0 - 0.9**10
SECOND_CORRECTION = 1.0 - 0.95**10
ADAM_EPSILON = 1e-08
NORM_EPSILON = 1e-05
SCORE_SCALE = 1.0 / math.sqrt(128)

MESH = pl.DeviceIdType.MESH
F32 = jnp.float32
BF16 = jnp.bfloat16

K_DEV = 2048
ROWS = 256
UNITS = 64
WIDTH = 16384


class Remote:
    def __init__(self, src, dst, sends, recvs, slot, device, arrives=None):
        self.copy = pltpu.make_async_remote_copy(
            src_ref=src, dst_ref=dst, send_sem=sends.at[slot], recv_sem=recvs.at[slot],
            device_id=device, device_id_type=MESH)
        arrives = dst if arrives is None else arrives
        self.inbound = pltpu.make_async_remote_copy(
            src_ref=arrives, dst_ref=arrives, send_sem=sends.at[slot], recv_sem=recvs.at[slot],
            device_id=device, device_id_type=MESH)
        self.copy.start()

    def sent(self):
        self.copy.wait_send()

    def came(self):
        self.inbound.wait_recv()


N_COPIES = 60


def step_kernel(
    clip_limit,
    grad_h, master_h, first_h, second_h, resid_h, gain_h, query_h, cache_h, fresh_h, length_h, table_h,
    first_o, second_o, attended_o, act_ref,
    g_v, ma_v, m_v, v_v, gf, gain_v, a_v, b_v, b_swap, c_s, c_r, h_s, h_r,
    p_s, p_r, t_s, t_r, s_g, q_v, kv_v, f_v, len_v, last, pick, length_ref, table_ref, load_sem, quarter_sem, sends, recvs, many,
):
    d = lax.axis_index("dp")
    t = lax.axis_index("tensor")
    x, zl, y = d // 8, (d // 4) % 2, d % 4
    zh, c = t // 2, t % 2
    oc = 1 - c
    xp, xq = x + 1 - 2 * (x % 2), (x + 3 + 2 * (x % 2)) % 4
    yp, yq = y + 1 - 2 * (y % 2), (y + 3 + 2 * (y % 2)) % 4

    def at(x_, zl_, y_, zh_=None, c_=None):
        zh_ = zh if zh_ is None else zh_
        c_ = c if c_ is None else c_
        return {"dp": x_ * 8 + zl_ * 4 + y_, "tensor": zh_ * 2 + c_}

    to_xp, to_yp, to_diag = at(xp, zl, y), at(x, zl, yp), at(xp, zl, yp)
    to_xq, to_yq, to_zl = at(xq, zl, y), at(x, zl, yq), at(x, 1 - zl, y)
    to_core = at(x, zl, y, zh, oc)

    near = [
        at(x_, z_, y_, zh, c_)
        for x_ in (x, xp) for y_ in (y, yp) for z_ in (zl, 1 - zl) for c_ in (c, oc)
    ][1:]
    far = [
        at(x_, 1 - zl if k == 2 else zl, y_, (zh + k) % 4, c)
        for x_ in (x, xq) for y_ in (y, yq) for k in range(4)
    ][1:]
    team = [at(x, zl, y, (zh + k // 2) % 4, (c + k) % 2) for k in range(1, 8)]

    loads = [
        None,
        pltpu.make_async_copy(resid_h, a_v.at[0, c], load_sem.at[1]),
        pltpu.make_async_copy(gain_h.at[pl.ds(pl.multiple_of(t * 16, 16), 16)], gain_v, load_sem.at[2]),
        pltpu.make_async_copy(master_h, ma_v, load_sem.at[3]),
        pltpu.make_async_copy(first_h, m_v, load_sem.at[4]),
        pltpu.make_async_copy(second_h, v_v, load_sem.at[5]),
        pltpu.make_async_copy(query_h, q_v, load_sem.at[6]),
        pltpu.make_async_copy(fresh_h, f_v, load_sem.at[7]),
        pltpu.make_async_copy(cache_h, kv_v, load_sem.at[8]),
        pltpu.make_async_copy(length_h, length_ref, load_sem.at[9]),
        pltpu.make_async_copy(table_h, table_ref, load_sem.at[10]),
    ]
    quarters = [
        pltpu.make_async_copy(
            grad_h.at[k // 2, pl.ds(k % 2 * 32, 32)], g_v.at[k // 2, pl.ds(k % 2 * 32, 32)], quarter_sem.at[k])
        for k in range(4)
    ]
    for quarter in quarters:
        quarter.start()
    loads[1].start()
    barrier = pltpu.get_barrier_semaphore()
    greeted = near + far + [team[k] for k in (2, 3, 4, 6)]
    for peer in greeted:
        pl.semaphore_signal(barrier, inc=1, device_id=peer, device_id_type=MESH)

    used = []

    def remote(src, dst, device, arrives=None):
        r = Remote(src, dst, sends, recvs, len(used), device, arrives)
        used.append(r)
        return r

    acc = jnp.zeros((8, K_DEV), F32)
    for k in range(4):
        quarters[k].wait()
        if k == 0:
            for load in loads[2:]:
                load.start()
        for r in range(2):
            rows = pl.ds(k % 2 * 32 + r * 16, 16)
            g = g_v[k // 2, rows, :].astype(F32)
            gf[k // 2, rows, :] = g
            sq = g * g
            acc += sq[:8] + sq[8:]
    local = jnp.sum(jnp.sum(acc, axis=0, keepdims=True), axis=1, keepdims=True)
    p_s[0] = jnp.broadcast_to(local, (1, 128))

    pl.semaphore_wait(barrier, len(greeted))

    def to_all(src, dst, peers, pair):
        for k, peer in enumerate(peers):
            pltpu.make_async_remote_copy(
                src_ref=src, dst_ref=dst.at[k], send_sem=many.at[pair], recv_sem=many.at[pair + 1],
                device_id=peer, device_id_type=MESH).start()

    def from_all(dst, pair):
        whole = pltpu.make_async_remote_copy(
            src_ref=dst, dst_ref=dst, send_sem=many.at[pair], recv_sem=many.at[pair + 1],
            device_id=to_core, device_id_type=MESH)
        whole.wait_send()
        whole.wait_recv()

    to_all(p_s.at[0], p_r.at[0], near, 0)

    loads[1].wait()
    def rows_of(slot, half, r):
        return a_v.at[slot, half, pl.ds(r * 128, 128)]

    def to_other_core(slot, r):
        return remote(rows_of(slot, c, r), rows_of(slot, c, r), to_core, rows_of(slot, oc, r))

    rows_x = [remote(rows_of(0, c, r), rows_of(1, c, r), to_xp) for r in range(2)]
    rows_y = [remote(rows_of(0, c, r), rows_of(2, c, r), to_yp) for r in range(2)]
    core_rows = [to_other_core(0, 0), to_other_core(0, 1)]

    def attend_block(g):
        rows = pl.ds(pl.multiple_of(g * 8, 8), 8)
        lane_row = lax.broadcasted_iota(jnp.int32, (32, 128), 1) // 16
        position = lax.broadcasted_iota(jnp.int32, (32, 128), 0).astype(F32)
        own_mine = (lax.broadcasted_iota(jnp.int32, (16, 128), 0)
                    == lax.broadcasted_iota(jnp.int32, (16, 128), 1) // 16)
        q = q_v[rows].reshape(128, 128)
        keys = kv_v[rows, 0].reshape(256, 128)
        values = kv_v[rows, 1].reshape(256, 128)
        own_key = f_v[rows, 0, 0:1].astype(F32).reshape(8, 128)
        own_value = f_v[rows, 0, 1:2].astype(F32).reshape(8, 128)
        own_key = jnp.concatenate([own_key, own_key], axis=0).astype(BF16)
        own_value = jnp.concatenate([own_value, own_value], axis=0).astype(BF16)
        every = lax.dot_general(keys, q, (((1,), (1,)), ((), ())), preferred_element_type=F32)
        own = lax.dot_general(own_key, q, (((1,), (1,)), ((), ())), preferred_element_type=F32)
        scores = every[:32]
        for r in range(1, 8):
            scores = jnp.where(lane_row == r, every[32 * r:32 * r + 32], scores)
        scores = jnp.where(position < len_v[pl.ds(g, 1), :], scores * SCORE_SCALE, -jnp.inf)
        own = jnp.sum(jnp.where(own_mine, own, 0.0), axis=0, keepdims=True) * SCORE_SCALE
        peak = jnp.maximum(jnp.max(scores, axis=0, keepdims=True), own)
        cached = jnp.exp(scores - peak)
        fresh_exp = jnp.exp(own - peak)
        inverse = 1.0 / (jnp.sum(cached, axis=0, keepdims=True) + fresh_exp)
        prob = cached * inverse
        own_prob = jnp.where(own_mine, fresh_exp * inverse, 0.0).astype(BF16)
        wide = jnp.concatenate([jnp.where(lane_row == r, prob, 0.0) for r in range(8)], axis=0).astype(BF16)
        out = lax.dot_general(wide, values, (((0,), (0,)), ((), ())), preferred_element_type=F32)
        out += lax.dot_general(own_prob, own_value, (((0,), (0,)), ((), ())), preferred_element_type=F32)
        attended_o[rows] = out.astype(BF16).reshape(8, 16, 128)

    def attend(first, last):
        @pl.loop(first // 4, last // 4)
        def _(g):
            for i in range(4):
                attend_block(4 * g + i)

    from_all(p_r.at[0], 0)
    total = p_s[0]
    for k in range(15):
        total += p_r[0, k]
    p_s[1] = total
    to_all(p_s.at[1], p_r.at[1], far, 2)

    ones = jnp.ones((8, 512), BF16)
    row_squares = jnp.zeros((8, ROWS), F32)
    for k in range(4):
        r = a_v[0, c, :, k * 512:(k + 1) * 512].astype(F32)
        sq = r * r
        high = sq.astype(BF16)
        low = (sq - high.astype(F32)).astype(BF16)
        for part in (high, low):
            row_squares += lax.dot_general(ones, part, (((1,), (1,)), ((), ())), preferred_element_type=F32)

    t_s[...] = row_squares[0:1, :]
    to_all(t_s, t_r, team, 4)

    for load in loads[6:]:
        load.wait()
    own_len = jnp.where(
        lax.broadcasted_iota(jnp.int32, (32, ROWS), 1) // 8
        == lax.broadcasted_iota(jnp.int32, (32, ROWS), 0),
        jnp.broadcast_to(length_ref[...].astype(F32), (32, ROWS)), 0.0).astype(BF16)
    spread_len = jnp.where(
        lax.broadcasted_iota(jnp.int32, (ROWS, 128), 0) % 8
        == lax.broadcasted_iota(jnp.int32, (ROWS, 128), 1) // 16, 1.0, 0.0).astype(BF16)
    len_v[...] = jnp.dot(own_len, spread_len, preferred_element_type=F32)
    attend(0, 8)

    from_all(p_r.at[1], 2)
    total = p_s[1]
    for k in range(15):
        total += p_r[1, k]
    clip = jnp.minimum(1.0, clip_limit / (jnp.sqrt(total) + CLIP_EPSILON))

    for load in loads[2:6]:
        load.wait()
    clip_one = clip[0:1, 0:1]
    gain = jnp.concatenate([gain_v[i:i + 1, :] for i in range(16)], axis=1)

    def fresh(parity, zone):
        row = pl.multiple_of((2 * zone + parity) * 8, 8)
        parts = []
        for i in range(2):
            clipped = gf[i, pl.ds(row, 8), :] * clip_one
            new_first = FIRST_DECAY * m_v[i, pl.ds(row, 8), :] + (1.0 - FIRST_DECAY) * clipped
            new_second = SECOND_DECAY * v_v[i, pl.ds(row, 8), :] + (1.0 - SECOND_DECAY) * clipped * clipped
            step = (new_first * (LEARN_RATE / FIRST_CORRECTION)) / (
                jnp.sqrt(new_second * (1.0 / SECOND_CORRECTION)) + ADAM_EPSILON)
            first_o[i, pl.ds(row, 8), :] = new_first
            second_o[i, pl.ds(row, 8), :] = new_second
            parts.append((ma_v[i, pl.ds(row, 8), :] - step) * gain)
        return jnp.concatenate(parts, axis=0).astype(BF16)

    @pl.loop(0, 4)
    def _(zone):
        b_v[0, c, pl.ds(pl.multiple_of(zone * 16, 16), 16), :] = fresh(c, zone)

    def units(src, dst, k, device):
        half = c if k == 0 else oc
        return remote(b_v.at[src, half], b_v.at[dst, half], device)

    unit = {}

    def units_out(k):
        unit[1, k] = units(0, 1, k, to_zl)
        unit[2, k] = units(0, 2, k, to_xq)
        unit[3, k] = units(0, 3, k, to_yq)

    units_out(0)

    @pl.loop(0, 4)
    def _(zone):
        b_swap[pl.ds(pl.multiple_of(zone * 16, 16), 16), :] = fresh(oc, zone)

    swap = remote(b_swap, b_v.at[0, c], to_core, b_v.at[0, oc])
    swap.came()
    units_out(1)

    spread = (lax.broadcasted_iota(jnp.int32, (32, 256), 0)
              == lax.broadcasted_iota(jnp.int32, (32, 256), 1) // 8).astype(F32).astype(BF16)
    table = jnp.broadcast_to(table_ref[...].astype(F32), (8, 32)).astype(BF16)
    wanted = jnp.dot(table, spread, preferred_element_type=F32)
    same_unit = (lax.broadcasted_iota(jnp.int32, (8, 256), 0)
                 == lax.broadcasted_iota(jnp.int32, (8, 256), 1) % 8)
    for group in range(4):
        gx, gy = (xp if group % 2 else x), (yp if group // 2 else y)
        for pair in range(4):
            halves = []
            for block in (2 * pair, 2 * pair + 1):
                bx = (gx + 3 + 2 * (gx % 2)) % 4 if block in (2, 4, 6, 7) else gx
                by = (gy + 3 + 2 * (gy % 2)) % 4 if block in (3, 5, 6, 7) else gy
                bz = 1 - zl if block in (1, 4, 5, 7) else zl
                shard = (bx * 8 + bz * 4 + by).astype(F32)
                halves.append(jnp.where(same_unit & (wanted == shard), 1.0, 0.0))
            row = group * 64 + pair * 16
            pick[row:row + 16, :] = jnp.concatenate(halves, axis=0).astype(BF16)

    from_all(t_r, 4)
    squares = t_s[...]
    for k in range(7):
        squares += t_r[k]
    s_g[0] = squares
    square_copies = [remote(s_g.at[0], s_g.at[slot], device) for slot, device in ((1, to_xp), (2, to_yp), (3, to_diag))]
    attend(8, 32)

    core_got = []
    diag = []

    def pass_rows(r):
        rows_x[r].came()
        core_got.append(to_other_core(1, r))
        if r == 0:
            diag.append(remote(rows_of(1, c, 0), rows_of(3, c, 0), to_yp))
        rows_y[r].came()
        core_got.append(to_other_core(2, r))
        if r == 1:
            diag.append(remote(rows_of(2, c, 1), rows_of(3, c, 1), to_xp))

    pass_rows(0)
    for k in range(2):
        unit[1, k].came()
        unit[4, k] = units(1, 4, k, to_xq)
        unit[5, k] = units(1, 5, k, to_yq)
    unit[2, 0].came()
    unit[6, 0] = units(2, 6, 0, to_yq)
    unit[3, 0].came()
    unit[3, 1].came()
    unit[6, 1] = units(3, 6, 1, to_xq)
    unit[2, 1].came()
    def half_product(slot, count, a, h):
        lhs = b_v[slot:slot + count, h].reshape(count * UNITS, K_DEV)
        return lax.dot_general(lhs, a_v[a, h], (((1,), (1,)), ((), ())), preferred_element_type=F32)

    def product(slot, count, a):
        out = half_product(slot, count, a, 0) + half_product(slot, count, a, 1)
        return out.reshape(count, 4, 16, ROWS).astype(BF16)

    def tile(p, pairs, a):
        out = product(2 * p, 2 * pairs, a)
        for i in range(pairs):
            for z in range(4):
                c_s[p + i, z, a] = out[2 * i:2 * i + 2, z]

    sums = []

    def send_sums(view_s, view_r):
        for k in range(1, 4):
            z = (zh + k) % 4
            sums.append(remote(view_s(z), view_r(k - 1), at(x, zl, y, z, c)))

    for r in core_rows:
        r.came()
    tile(0, 2, 0)
    send_sums(lambda z: c_s.at[pl.ds(0, 2), z, 0], lambda k: c_r.at[k, pl.ds(0, 2), 0])
    pass_rows(1)
    for r in core_got:
        r.came()

    for a in (1, 2):
        tile(0, 2, a)

    send_sums(lambda z: c_s.at[pl.ds(0, 2), z, pl.ds(1, 2)], lambda k: c_r.at[k, pl.ds(0, 2), pl.ds(1, 2)])
    unit[4, 0].came()
    unit[7, 0] = units(4, 7, 0, to_yq)
    unit[5, 0].came()
    unit[5, 1].came()
    unit[7, 1] = units(5, 7, 1, to_xq)
    unit[4, 1].came()

    for a in range(3):
        tile(2, 1, a)

    send_sums(lambda z: c_s.at[2, z, pl.ds(0, 3)], lambda k: c_r.at[k, 2, pl.ds(0, 3)])
    last_rows = []
    for r in range(2):
        diag[r].came()
        last_rows.append(to_other_core(3, r))
    for r in last_rows:
        r.came()
    tile(0, 2, 3)
    tile(2, 1, 3)
    send_sums(lambda z: c_s.at[pl.ds(0, 3), z, 3], lambda k: c_r.at[k, pl.ds(0, 3), 3])

    for k in range(2):
        unit[6, k].came()

    for a in range(4):
        out = product(6, 1, a)
        for z in range(4):
            c_s[3, z, a, 0] = out[0, z]

    send_sums(lambda z: c_s.at[3, z, :, 0], lambda k: c_r.at[k, 3, :, 0])

    unit[7, 0].came()

    for a in range(4):
        last[a] = half_product(7, 1, a, c)

    unit[7, 1].came()

    def finish_two(first):
        for a in (first + 1, first):
            out = (last[a] + half_product(7, 1, a, oc)).reshape(4, 16, ROWS).astype(BF16)
            for z in range(4):
                c_s[3, z, a, 1] = out[z]
        send_sums(
            lambda z: c_s.at[3, z, pl.ds(first, 2), 1], lambda k: c_r.at[k, 3, pl.ds(first, 2), 1])

    finish_two(2)
    finish_two(0)

    for r in square_copies:
        r.came()

    def activations(a, p):
        scale = lax.rsqrt(s_g[a] * (1.0 / WIDTH) + NORM_EPSILON)
        v = c_s[p, zh, a].astype(F32)
        for k in range(3):
            v += c_r[k, p, a].astype(F32)
        gate = v[:, :8] * scale
        up = v[:, 8:] * scale
        hidden = (gate / (1.0 + jnp.exp(-gate)) * up).reshape(16, ROWS).astype(BF16)
        h_s[a, p * 16:(p + 1) * 16, :] = hidden

    for r in sums[:12]:
        r.came()
    outs = []
    for a, device in ((3, to_diag), (1, to_xp), (2, to_yp), (0, None)):
        for p in range(3):
            activations(a, p)
        if device is not None:
            outs.append(remote(h_s.at[a, pl.ds(0, 48)], h_r.at[a, pl.ds(0, 48)], device))
    def last_part(a, device):
        activations(a, 3)
        if device is not None:
            outs.append(remote(h_s.at[a, pl.ds(48, 16)], h_r.at[a, pl.ds(48, 16)], device))

    for r in sums[12:18]:
        r.came()
    last_part(3, to_diag)
    last_part(2, to_yp)
    for r in sums[18:]:
        r.came()
    last_part(1, to_xp)
    last_part(0, None)
    h_r[0] = h_s[0]
    for r in outs:
        r.came()
    act_ref[...] = lax.dot_general(
        h_r[...].reshape(256, ROWS), pick[...], (((0,), (0,)), ((), ())), preferred_element_type=F32).astype(BF16)

    for r in used:
        r.sent()
    assert len(used) <= N_COPIES, len(used)


def step(gradient, master, first_moment, second_moment, residual, norm_gain,
         queries, layer_cache, fresh_entries, lengths, shard_table, clip_limit):
    hbm = pl.BlockSpec(memory_space=pl.ANY)
    vmem = pl.BlockSpec(memory_space=pltpu.VMEM)
    slab = gradient.shape

    def kernel(*refs):
        step_kernel(clip_limit, *refs)

    results = pl.pallas_call(
        kernel,
        out_shape=(
            pltpu.VMEM(slab, F32),
            pltpu.VMEM(slab, F32),
            pltpu.VMEM(queries.shape, BF16),
            pltpu.VMEM((ROWS, 256), BF16),
        ),
        in_specs=[hbm] * 11,
        out_specs=(vmem,) * 4,
        scratch_shapes=[
            pltpu.VMEM(slab, BF16),
            pltpu.VMEM(slab, F32),
            pltpu.VMEM(slab, F32),
            pltpu.VMEM(slab, F32),
            pltpu.VMEM(slab, F32),
            pltpu.VMEM((16, 128), F32),
            pltpu.VMEM((4, 2, ROWS, K_DEV), BF16),
            pltpu.VMEM((8, 2, UNITS, K_DEV), BF16),
            pltpu.VMEM((UNITS, K_DEV), BF16),
            pltpu.VMEM((4, 4, 4, 2, 16, ROWS), BF16),
            pltpu.VMEM((3, 4, 4, 2, 16, ROWS), BF16),
            pltpu.VMEM((4, UNITS, ROWS), BF16),
            pltpu.VMEM((4, UNITS, ROWS), BF16),
            pltpu.VMEM((2, 1, 128), F32),
            pltpu.VMEM((2, 15, 1, 128), F32),
            pltpu.VMEM((1, ROWS), F32),
            pltpu.VMEM((7, 1, ROWS), F32),
            pltpu.VMEM((4, 1, ROWS), F32),
            pltpu.VMEM(queries.shape, BF16),
            pltpu.VMEM((ROWS, 2, 32, 128), BF16),
            pltpu.VMEM((ROWS, 1, 2, 128), BF16),
            pltpu.VMEM((32, 128), F32),
            pltpu.VMEM((4, UNITS, ROWS), F32),
            pltpu.VMEM((256, 256), BF16),
            pltpu.VMEM((1, ROWS), jnp.int32),
            pltpu.VMEM((1, 32), jnp.int32),
            pltpu.SemaphoreType.DMA((11,)),
            pltpu.SemaphoreType.DMA((4,)),
            pltpu.SemaphoreType.DMA((N_COPIES,)),
            pltpu.SemaphoreType.DMA((N_COPIES,)),
            pltpu.SemaphoreType.DMA((6,)),
        ],
        compiler_params=pltpu.CompilerParams(
            collective_id=0, has_side_effects=True, vmem_limit_bytes=56 << 20),
        name="step",
    )(gradient, master, first_moment, second_moment, residual,
      norm_gain.reshape(128, 128), queries, layer_cache.reshape(ROWS, 2, 32, 128),
      fresh_entries.transpose(0, 2, 1, 3), lengths.reshape(1, ROWS), shard_table.reshape(1, 32))

    def write(*refs):
        copies = [pltpu.make_async_copy(refs[i], refs[4 + i], refs[8].at[i]) for i in range(4)]
        for copy in copies:
            copy.start()
        for copy in copies:
            copy.wait()

    return pl.pallas_call(
        write,
        out_shape=[jax.ShapeDtypeStruct(r.shape, r.dtype) for r in results],
        in_specs=[vmem] * 4,
        out_specs=[hbm] * 4,
        scratch_shapes=[pltpu.SemaphoreType.DMA((4,))],
        name="write",
    )(*[pltpu.with_memory_space_constraint(r, pltpu.VMEM) for r in results])


def per_device(gradient, master, first_moment, second_moment, residual, norm_gain,
               queries, layer_cache, fresh_entries, lengths, shard_table):
    entry_count = gradient.size * lax.axis_size("dp") * lax.axis_size("tensor")
    return step(
        gradient, master, first_moment, second_moment, residual, norm_gain,
        queries, layer_cache, fresh_entries, lengths, shard_table,
        CLIP_LEVEL * math.sqrt(entry_count))


def solution(mesh):
    return jax.shard_map(
        per_device,
        mesh=mesh,
        in_specs=(
            P(None, "dp", "tensor"),
            P(None, "dp", "tensor"),
            P(None, "dp", "tensor"),
            P(None, "dp", "tensor"),
            P("dp", "tensor"),
            P(),
            P("dp", "tensor", None),
            P("dp", None, "tensor", None, None),
            P("dp", None, "tensor", None),
            P("dp"),
            P(),
        ),
        out_specs=(
            P(None, "dp", "tensor"),
            P(None, "dp", "tensor"),
            P("dp", "tensor", None),
            P("dp", "tensor"),
        ),
        check_vma=False,
    )
```

```python
import math

import jax
import jax.numpy as jnp
from jax import lax
from jax.experimental import pallas as pl
from jax.experimental.pallas import tpu as pltpu
from jax.sharding import PartitionSpec as P

LEARN_RATE = 0.001
CLIP_LEVEL = 0.5
CLIP_EPSILON = 1e-06
FIRST_DECAY = 0.9
SECOND_DECAY = 0.95
FIRST_CORRECTION = 1.0 - 0.9**10
SECOND_CORRECTION = 1.0 - 0.95**10
ADAM_EPSILON = 1e-08
NORM_EPSILON = 1e-05
SCORE_SCALE = 1.0 / math.sqrt(128)

MESH = pl.DeviceIdType.MESH
F32 = jnp.float32
BF16 = jnp.bfloat16

K_DEV = 2048
ROWS = 256
UNITS = 64
WIDTH = 16384


class Remote:
    def __init__(self, src, dst, sends, recvs, slot, device, arrives=None):
        self.copy = pltpu.make_async_remote_copy(
            src_ref=src, dst_ref=dst, send_sem=sends.at[slot], recv_sem=recvs.at[slot],
            device_id=device, device_id_type=MESH)
        arrives = dst if arrives is None else arrives
        self.inbound = pltpu.make_async_remote_copy(
            src_ref=arrives, dst_ref=arrives, send_sem=sends.at[slot], recv_sem=recvs.at[slot],
            device_id=device, device_id_type=MESH)
        self.copy.start()

    def sent(self):
        self.copy.wait_send()

    def came(self):
        self.inbound.wait_recv()


N_COPIES = 60


def step_kernel(
    clip_limit,
    grad_h, master_h, first_h, second_h, resid_h, gain_h, query_h, cache_h, fresh_h, length_h, table_h,
    first_o, second_o, attended_o, act_ref,
    g_v, ma_v, m_v, v_v, gf, gain_v, a_v, b_v, b_swap, c_s, c_r, h_s, h_r,
    p_s, p_r, t_s, t_r, s_g, q_v, kv_v, f_v, len_v, last, pick, length_ref, table_ref, load_sem, quarter_sem, sends, recvs, many,
):
    d = lax.axis_index("dp")
    t = lax.axis_index("tensor")
    x, zl, y = d // 8, (d // 4) % 2, d % 4
    zh, c = t // 2, t % 2
    oc = 1 - c
    xp, xq = x + 1 - 2 * (x % 2), (x + 3 + 2 * (x % 2)) % 4
    yp, yq = y + 1 - 2 * (y % 2), (y + 3 + 2 * (y % 2)) % 4

    def at(x_, zl_, y_, zh_=None, c_=None):
        zh_ = zh if zh_ is None else zh_
        c_ = c if c_ is None else c_
        return {"dp": x_ * 8 + zl_ * 4 + y_, "tensor": zh_ * 2 + c_}

    to_xp, to_yp, to_diag = at(xp, zl, y), at(x, zl, yp), at(xp, zl, yp)
    to_xq, to_yq, to_zl = at(xq, zl, y), at(x, zl, yq), at(x, 1 - zl, y)
    to_core = at(x, zl, y, zh, oc)

    near = [
        at(x_, z_, y_, zh, c_)
        for x_ in (x, xp) for y_ in (y, yp) for z_ in (zl, 1 - zl) for c_ in (c, oc)
    ][1:]
    far = [
        at(x_, 1 - zl if k == 2 else zl, y_, (zh + k) % 4, c)
        for x_ in (x, xq) for y_ in (y, yq) for k in range(4)
    ][1:]
    team = [at(x, zl, y, (zh + k // 2) % 4, (c + k) % 2) for k in range(1, 8)]

    loads = [
        None,
        pltpu.make_async_copy(resid_h, a_v.at[0, c], load_sem.at[1]),
        pltpu.make_async_copy(gain_h.at[pl.ds(pl.multiple_of(t * 16, 16), 16)], gain_v, load_sem.at[2]),
        pltpu.make_async_copy(master_h, ma_v, load_sem.at[3]),
        pltpu.make_async_copy(first_h, m_v, load_sem.at[4]),
        pltpu.make_async_copy(second_h, v_v, load_sem.at[5]),
        pltpu.make_async_copy(query_h, q_v, load_sem.at[6]),
        pltpu.make_async_copy(fresh_h, f_v, load_sem.at[7]),
        pltpu.make_async_copy(cache_h, kv_v, load_sem.at[8]),
        pltpu.make_async_copy(length_h, length_ref, load_sem.at[9]),
        pltpu.make_async_copy(table_h, table_ref, load_sem.at[10]),
    ]
    quarters = [
        pltpu.make_async_copy(
            grad_h.at[k // 2, pl.ds(k % 2 * 32, 32)], g_v.at[k // 2, pl.ds(k % 2 * 32, 32)], quarter_sem.at[k])
        for k in range(4)
    ]
    for quarter in quarters:
        quarter.start()
    loads[1].start()
    barrier = pltpu.get_barrier_semaphore()
    greeted = near + far + [team[k] for k in (2, 3, 4, 6)]
    for peer in greeted:
        pl.semaphore_signal(barrier, inc=1, device_id=peer, device_id_type=MESH)

    used = []

    def remote(src, dst, device, arrives=None):
        r = Remote(src, dst, sends, recvs, len(used), device, arrives)
        used.append(r)
        return r

    acc = jnp.zeros((8, K_DEV), F32)
    for k in range(4):
        quarters[k].wait()
        if k == 0:
            for load in loads[2:]:
                load.start()
        for r in range(2):
            rows = pl.ds(k % 2 * 32 + r * 16, 16)
            g = g_v[k // 2, rows, :].astype(F32)
            gf[k // 2, rows, :] = g
            sq = g * g
            acc += sq[:8] + sq[8:]
    local = jnp.sum(jnp.sum(acc, axis=0, keepdims=True), axis=1, keepdims=True)
    p_s[0] = jnp.broadcast_to(local, (1, 128))

    pl.semaphore_wait(barrier, len(greeted))

    def to_all(src, dst, peers, pair):
        for k, peer in enumerate(peers):
            pltpu.make_async_remote_copy(
                src_ref=src, dst_ref=dst.at[k], send_sem=many.at[pair], recv_sem=many.at[pair + 1],
                device_id=peer, device_id_type=MESH).start()

    def from_all(dst, pair):
        whole = pltpu.make_async_remote_copy(
            src_ref=dst, dst_ref=dst, send_sem=many.at[pair], recv_sem=many.at[pair + 1],
            device_id=to_core, device_id_type=MESH)
        whole.wait_send()
        whole.wait_recv()

    to_all(p_s.at[0], p_r.at[0], near, 0)

    loads[1].wait()
    def rows_of(slot, half, r):
        return a_v.at[slot, half, pl.ds(r * 128, 128)]

    def to_other_core(slot, r):
        return remote(rows_of(slot, c, r), rows_of(slot, c, r), to_core, rows_of(slot, oc, r))

    rows_x = [remote(rows_of(0, c, r), rows_of(1, c, r), to_xp) for r in range(2)]
    rows_y = [remote(rows_of(0, c, r), rows_of(2, c, r), to_yp) for r in range(2)]
    core_rows = [to_other_core(0, 0), to_other_core(0, 1)]

    def attend_block(g):
        rows = pl.ds(pl.multiple_of(g * 8, 8), 8)
        lane_row = lax.broadcasted_iota(jnp.int32, (32, 128), 1) // 16
        position = lax.broadcasted_iota(jnp.int32, (32, 128), 0).astype(F32)
        own_mine = (lax.broadcasted_iota(jnp.int32, (16, 128), 0)
                    == lax.broadcasted_iota(jnp.int32, (16, 128), 1) // 16)
        q = q_v[rows].reshape(128, 128)
        keys = kv_v[rows, 0].reshape(256, 128)
        values = kv_v[rows, 1].reshape(256, 128)
        own_key = f_v[rows, 0, 0:1].astype(F32).reshape(8, 128)
        own_value = f_v[rows, 0, 1:2].astype(F32).reshape(8, 128)
        own_key = jnp.concatenate([own_key, own_key], axis=0).astype(BF16)
        own_value = jnp.concatenate([own_value, own_value], axis=0).astype(BF16)
        every = lax.dot_general(keys, q, (((1,), (1,)), ((), ())), preferred_element_type=F32)
        own = lax.dot_general(own_key, q, (((1,), (1,)), ((), ())), preferred_element_type=F32)
        scores = every[:32]
        for r in range(1, 8):
            scores = jnp.where(lane_row == r, every[32 * r:32 * r + 32], scores)
        scores = jnp.where(position < len_v[pl.ds(g, 1), :], scores * SCORE_SCALE, -jnp.inf)
        own = jnp.sum(jnp.where(own_mine, own, 0.0), axis=0, keepdims=True) * SCORE_SCALE
        peak = jnp.maximum(jnp.max(scores, axis=0, keepdims=True), own)
        cached = jnp.exp(scores - peak)
        fresh_exp = jnp.exp(own - peak)
        inverse = 1.0 / (jnp.sum(cached, axis=0, keepdims=True) + fresh_exp)
        prob = cached * inverse
        own_prob = jnp.where(own_mine, fresh_exp * inverse, 0.0).astype(BF16)
        wide = jnp.concatenate([jnp.where(lane_row == r, prob, 0.0) for r in range(8)], axis=0).astype(BF16)
        out = lax.dot_general(wide, values, (((0,), (0,)), ((), ())), preferred_element_type=F32)
        out += lax.dot_general(own_prob, own_value, (((0,), (0,)), ((), ())), preferred_element_type=F32)
        attended_o[rows] = out.astype(BF16).reshape(8, 16, 128)

    def attend(first, last):
        @pl.loop(first // 4, last // 4)
        def _(g):
            for i in range(4):
                attend_block(4 * g + i)

    from_all(p_r.at[0], 0)
    total = p_s[0]
    for k in range(15):
        total += p_r[0, k]
    p_s[1] = total
    to_all(p_s.at[1], p_r.at[1], far, 2)

    ones = jnp.ones((8, 512), BF16)
    row_squares = jnp.zeros((8, ROWS), F32)
    for k in range(4):
        r = a_v[0, c, :, k * 512:(k + 1) * 512].astype(F32)
        sq = r * r
        high = sq.astype(BF16)
        low = (sq - high.astype(F32)).astype(BF16)
        for part in (high, low):
            row_squares += lax.dot_general(ones, part, (((1,), (1,)), ((), ())), preferred_element_type=F32)

    t_s[...] = row_squares[0:1, :]
    to_all(t_s, t_r, team, 4)


    from_all(p_r.at[1], 2)
    total = p_s[1]
    for k in range(15):
        total += p_r[1, k]
    clip = jnp.minimum(1.0, clip_limit / (jnp.sqrt(total) + CLIP_EPSILON))

    for load in loads[2:6]:
        load.wait()
    clip_one = clip[0:1, 0:1]
    gain = jnp.concatenate([gain_v[i:i + 1, :] for i in range(16)], axis=1)

    def fresh(parity, zone):
        row = pl.multiple_of((2 * zone + parity) * 8, 8)
        parts = []
        for i in range(2):
            clipped = gf[i, pl.ds(row, 8), :] * clip_one
            new_first = FIRST_DECAY * m_v[i, pl.ds(row, 8), :] + (1.0 - FIRST_DECAY) * clipped
            new_second = SECOND_DECAY * v_v[i, pl.ds(row, 8), :] + (1.0 - SECOND_DECAY) * clipped * clipped
            step = (new_first * (LEARN_RATE / FIRST_CORRECTION)) / (
                jnp.sqrt(new_second * (1.0 / SECOND_CORRECTION)) + ADAM_EPSILON)
            first_o[i, pl.ds(row, 8), :] = new_first
            second_o[i, pl.ds(row, 8), :] = new_second
            parts.append((ma_v[i, pl.ds(row, 8), :] - step) * gain)
        return jnp.concatenate(parts, axis=0).astype(BF16)

    @pl.loop(0, 4)
    def _(zone):
        b_v[0, c, pl.ds(pl.multiple_of(zone * 16, 16), 16), :] = fresh(c, zone)

    def units(src, dst, k, device):
        half = c if k == 0 else oc
        return remote(b_v.at[src, half], b_v.at[dst, half], device)

    unit = {}

    def units_out(k):
        unit[1, k] = units(0, 1, k, to_zl)
        unit[2, k] = units(0, 2, k, to_xq)
        unit[3, k] = units(0, 3, k, to_yq)

    units_out(0)

    @pl.loop(0, 4)
    def _(zone):
        b_swap[pl.ds(pl.multiple_of(zone * 16, 16), 16), :] = fresh(oc, zone)

    swap = remote(b_swap, b_v.at[0, c], to_core, b_v.at[0, oc])
    swap.came()
    units_out(1)

    for load in loads[6:]:
        load.wait()
    own_len = jnp.where(
        lax.broadcasted_iota(jnp.int32, (32, ROWS), 1) // 8
        == lax.broadcasted_iota(jnp.int32, (32, ROWS), 0),
        jnp.broadcast_to(length_ref[...].astype(F32), (32, ROWS)), 0.0).astype(BF16)
    spread_len = jnp.where(
        lax.broadcasted_iota(jnp.int32, (ROWS, 128), 0) % 8
        == lax.broadcasted_iota(jnp.int32, (ROWS, 128), 1) // 16, 1.0, 0.0).astype(BF16)
    len_v[...] = jnp.dot(own_len, spread_len, preferred_element_type=F32)

    spread = (lax.broadcasted_iota(jnp.int32, (32, 256), 0)
              == lax.broadcasted_iota(jnp.int32, (32, 256), 1) // 8).astype(F32).astype(BF16)
    table = jnp.broadcast_to(table_ref[...].astype(F32), (8, 32)).astype(BF16)
    wanted = jnp.dot(table, spread, preferred_element_type=F32)
    same_unit = (lax.broadcasted_iota(jnp.int32, (8, 256), 0)
                 == lax.broadcasted_iota(jnp.int32, (8, 256), 1) % 8)
    for group in range(4):
        gx, gy = (xp if group % 2 else x), (yp if group // 2 else y)
        for pair in range(4):
            halves = []
            for block in (2 * pair, 2 * pair + 1):
                bx = (gx + 3 + 2 * (gx % 2)) % 4 if block in (2, 4, 6, 7) else gx
                by = (gy + 3 + 2 * (gy % 2)) % 4 if block in (3, 5, 6, 7) else gy
                bz = 1 - zl if block in (1, 4, 5, 7) else zl
                shard = (bx * 8 + bz * 4 + by).astype(F32)
                halves.append(jnp.where(same_unit & (wanted == shard), 1.0, 0.0))
            row = group * 64 + pair * 16
            pick[row:row + 16, :] = jnp.concatenate(halves, axis=0).astype(BF16)

    from_all(t_r, 4)
    squares = t_s[...]
    for k in range(7):
        squares += t_r[k]
    s_g[0] = squares
    square_copies = [remote(s_g.at[0], s_g.at[slot], device) for slot, device in ((1, to_xp), (2, to_yp), (3, to_diag))]
    attend(0, 32)

    core_got = []
    diag = []

    def pass_rows(r):
        rows_x[r].came()
        core_got.append(to_other_core(1, r))
        if r == 0:
            diag.append(remote(rows_of(1, c, 0), rows_of(3, c, 0), to_yp))
        rows_y[r].came()
        core_got.append(to_other_core(2, r))
        if r == 1:
            diag.append(remote(rows_of(2, c, 1), rows_of(3, c, 1), to_xp))

    pass_rows(0)
    for k in range(2):
        unit[1, k].came()
        unit[4, k] = units(1, 4, k, to_xq)
        unit[5, k] = units(1, 5, k, to_yq)
    unit[2, 0].came()
    unit[6, 0] = units(2, 6, 0, to_yq)
    unit[3, 0].came()
    unit[3, 1].came()
    unit[6, 1] = units(3, 6, 1, to_xq)
    unit[2, 1].came()
    def half_product(slot, count, a, h):
        lhs = b_v[slot:slot + count, h].reshape(count * UNITS, K_DEV)
        return lax.dot_general(lhs, a_v[a, h], (((1,), (1,)), ((), ())), preferred_element_type=F32)

    def product(slot, count, a):
        out = half_product(slot, count, a, 0) + half_product(slot, count, a, 1)
        return out.reshape(count, 4, 16, ROWS).astype(BF16)

    def tile(p, pairs, a):
        out = product(2 * p, 2 * pairs, a)
        for i in range(pairs):
            for z in range(4):
                c_s[p + i, z, a] = out[2 * i:2 * i + 2, z]

    sums = []

    def send_sums(view_s, view_r):
        for k in range(1, 4):
            z = (zh + k) % 4
            sums.append(remote(view_s(z), view_r(k - 1), at(x, zl, y, z, c)))

    for r in core_rows:
        r.came()
    tile(0, 2, 0)
    send_sums(lambda z: c_s.at[pl.ds(0, 2), z, 0], lambda k: c_r.at[k, pl.ds(0, 2), 0])
    pass_rows(1)
    for r in core_got:
        r.came()

    for a in (1, 2):
        tile(0, 2, a)

    send_sums(lambda z: c_s.at[pl.ds(0, 2), z, pl.ds(1, 2)], lambda k: c_r.at[k, pl.ds(0, 2), pl.ds(1, 2)])
    unit[4, 0].came()
    unit[7, 0] = units(4, 7, 0, to_yq)
    unit[5, 0].came()
    unit[5, 1].came()
    unit[7, 1] = units(5, 7, 1, to_xq)
    unit[4, 1].came()

    for a in range(3):
        tile(2, 1, a)

    send_sums(lambda z: c_s.at[2, z, pl.ds(0, 3)], lambda k: c_r.at[k, 2, pl.ds(0, 3)])
    last_rows = []
    for r in range(2):
        diag[r].came()
        last_rows.append(to_other_core(3, r))
    for r in last_rows:
        r.came()
    tile(0, 2, 3)
    tile(2, 1, 3)
    send_sums(lambda z: c_s.at[pl.ds(0, 3), z, 3], lambda k: c_r.at[k, pl.ds(0, 3), 3])

    for k in range(2):
        unit[6, k].came()

    for a in range(4):
        out = product(6, 1, a)
        for z in range(4):
            c_s[3, z, a, 0] = out[0, z]

    send_sums(lambda z: c_s.at[3, z, :, 0], lambda k: c_r.at[k, 3, :, 0])

    unit[7, 0].came()

    for a in range(4):
        last[a] = half_product(7, 1, a, c)

    unit[7, 1].came()

    def finish_two(first):
        for a in (first + 1, first):
            out = (last[a] + half_product(7, 1, a, oc)).reshape(4, 16, ROWS).astype(BF16)
            for z in range(4):
                c_s[3, z, a, 1] = out[z]
        send_sums(
            lambda z: c_s.at[3, z, pl.ds(first, 2), 1], lambda k: c_r.at[k, 3, pl.ds(first, 2), 1])

    finish_two(2)
    finish_two(0)

    for r in square_copies:
        r.came()

    def activations(a, p):
        scale = lax.rsqrt(s_g[a] * (1.0 / WIDTH) + NORM_EPSILON)
        v = c_s[p, zh, a].astype(F32)
        for k in range(3):
            v += c_r[k, p, a].astype(F32)
        gate = v[:, :8] * scale
        up = v[:, 8:] * scale
        hidden = (gate / (1.0 + jnp.exp(-gate)) * up).reshape(16, ROWS).astype(BF16)
        h_s[a, p * 16:(p + 1) * 16, :] = hidden

    for r in sums[:12]:
        r.came()
    outs = []
    for a, device in ((3, to_diag), (1, to_xp), (2, to_yp), (0, None)):
        for p in range(3):
            activations(a, p)
        if device is not None:
            outs.append(remote(h_s.at[a, pl.ds(0, 48)], h_r.at[a, pl.ds(0, 48)], device))
    def last_part(a, device):
        activations(a, 3)
        if device is not None:
            outs.append(remote(h_s.at[a, pl.ds(48, 16)], h_r.at[a, pl.ds(48, 16)], device))

    for r in sums[12:18]:
        r.came()
    last_part(3, to_diag)
    last_part(2, to_yp)
    for r in sums[18:]:
        r.came()
    last_part(1, to_xp)
    last_part(0, None)
    h_r[0] = h_s[0]
    for r in outs:
        r.came()
    act_ref[...] = lax.dot_general(
        h_r[...].reshape(256, ROWS), pick[...], (((0,), (0,)), ((), ())), preferred_element_type=F32).astype(BF16)

    for r in used:
        r.sent()
    assert len(used) <= N_COPIES, len(used)


def step(gradient, master, first_moment, second_moment, residual, norm_gain,
         queries, layer_cache, fresh_entries, lengths, shard_table, clip_limit):
    hbm = pl.BlockSpec(memory_space=pl.ANY)
    vmem = pl.BlockSpec(memory_space=pltpu.VMEM)
    slab = gradient.shape

    def kernel(*refs):
        step_kernel(clip_limit, *refs)

    results = pl.pallas_call(
        kernel,
        out_shape=(
            pltpu.VMEM(slab, F32),
            pltpu.VMEM(slab, F32),
            pltpu.VMEM(queries.shape, BF16),
            pltpu.VMEM((ROWS, 256), BF16),
        ),
        in_specs=[hbm] * 11,
        out_specs=(vmem,) * 4,
        scratch_shapes=[
            pltpu.VMEM(slab, BF16),
            pltpu.VMEM(slab, F32),
            pltpu.VMEM(slab, F32),
            pltpu.VMEM(slab, F32),
            pltpu.VMEM(slab, F32),
            pltpu.VMEM((16, 128), F32),
            pltpu.VMEM((4, 2, ROWS, K_DEV), BF16),
            pltpu.VMEM((8, 2, UNITS, K_DEV), BF16),
            pltpu.VMEM((UNITS, K_DEV), BF16),
            pltpu.VMEM((4, 4, 4, 2, 16, ROWS), BF16),
            pltpu.VMEM((3, 4, 4, 2, 16, ROWS), BF16),
            pltpu.VMEM((4, UNITS, ROWS), BF16),
            pltpu.VMEM((4, UNITS, ROWS), BF16),
            pltpu.VMEM((2, 1, 128), F32),
            pltpu.VMEM((2, 15, 1, 128), F32),
            pltpu.VMEM((1, ROWS), F32),
            pltpu.VMEM((7, 1, ROWS), F32),
            pltpu.VMEM((4, 1, ROWS), F32),
            pltpu.VMEM(queries.shape, BF16),
            pltpu.VMEM((ROWS, 2, 32, 128), BF16),
            pltpu.VMEM((ROWS, 1, 2, 128), BF16),
            pltpu.VMEM((32, 128), F32),
            pltpu.VMEM((4, UNITS, ROWS), F32),
            pltpu.VMEM((256, 256), BF16),
            pltpu.VMEM((1, ROWS), jnp.int32),
            pltpu.VMEM((1, 32), jnp.int32),
            pltpu.SemaphoreType.DMA((11,)),
            pltpu.SemaphoreType.DMA((4,)),
            pltpu.SemaphoreType.DMA((N_COPIES,)),
            pltpu.SemaphoreType.DMA((N_COPIES,)),
            pltpu.SemaphoreType.DMA((6,)),
        ],
        compiler_params=pltpu.CompilerParams(
            collective_id=0, has_side_effects=True, vmem_limit_bytes=56 << 20),
        name="step",
    )(gradient, master, first_moment, second_moment, residual,
      norm_gain.reshape(128, 128), queries, layer_cache.reshape(ROWS, 2, 32, 128),
      fresh_entries.transpose(0, 2, 1, 3), lengths.reshape(1, ROWS), shard_table.reshape(1, 32))

    def write(*refs):
        copies = [pltpu.make_async_copy(refs[i], refs[4 + i], refs[8].at[i]) for i in range(4)]
        for copy in copies:
            copy.start()
        for copy in copies:
            copy.wait()

    return pl.pallas_call(
        write,
        out_shape=[jax.ShapeDtypeStruct(r.shape, r.dtype) for r in results],
        in_specs=[vmem] * 4,
        out_specs=[hbm] * 4,
        scratch_shapes=[pltpu.SemaphoreType.DMA((4,))],
        name="write",
    )(*[pltpu.with_memory_space_constraint(r, pltpu.VMEM) for r in results])


def per_device(gradient, master, first_moment, second_moment, residual, norm_gain,
               queries, layer_cache, fresh_entries, lengths, shard_table):
    entry_count = gradient.size * lax.axis_size("dp") * lax.axis_size("tensor")
    return step(
        gradient, master, first_moment, second_moment, residual, norm_gain,
        queries, layer_cache, fresh_entries, lengths, shard_table,
        CLIP_LEVEL * math.sqrt(entry_count))


def solution(mesh):
    return jax.shard_map(
        per_device,
        mesh=mesh,
        in_specs=(
            P(None, "dp", "tensor"),
            P(None, "dp", "tensor"),
            P(None, "dp", "tensor"),
            P(None, "dp", "tensor"),
            P("dp", "tensor"),
            P(),
            P("dp", "tensor", None),
            P("dp", None, "tensor", None, None),
            P("dp", None, "tensor", None),
            P("dp"),
            P(),
        ),
        out_specs=(
            P(None, "dp", "tensor"),
            P(None, "dp", "tensor"),
            P("dp", "tensor", None),
            P("dp", "tensor"),
        ),
        check_vma=False,
    )
```
